32 devices in a mesh: tm: 8 (over z, x), rows: 4 (over y, core).
Axes of the slice: x: 2, y: 2, z: 4, core: 2. Of those that a mesh axis runs over, the one named last changes fastest.
Arguments:
- features: float32 [262144, 512], P(('tm', 'rows'))
- response_lines: float32 [262144, 128], P(('tm', 'rows'))
- row_counts: int32 [8], replicated, may hold values from 16384 to 32768, as said below
- ridge_codes: int32 [8], replicated, may hold values from 2 to 33
Outputs:
- forecast: bfloat16 [262144, 128], P(('tm', 'rows'))
- partition_mse: float32 [8], P('tm')
The draws below stay inside these ranges and needn't reach their ends.
Inputs may be any that keep to these rules, and one draw needn't show every extreme that they name: `row_counts`: each count is a multiple of 128, at least half of 32768 and at most 32768.
All inputs are finite; a program needn't handle non-finite values.
Results may differ from the reference program's by a relative error of at most 0.001.
Values sent between devices are 32-bit elements; how exact they have to be, the bound alone decides.
No kernel may reach another device: no remote copies, remote signals or barrier semaphores. Data moves between devices by JAX's collectives and lax.ppermute only.
A program may use at most 128 MiB of HBM per device.

```python
import math
import jax
import jax.numpy as jnp
from jax import lax

F = 512
RESPONSE_COUNT = 128
SHARD = 32768
OVERALL_LINES = 262144
N_TM = 8


def joint_rows(key):
    base = jax.random.fold_in(key, 71)
    key_feat, key_coef, key_noise = jax.random.split(base, 3)
    feats = jax.random.normal(key_feat, (OVERALL_LINES, F), jnp.float32)
    coefs = jax.random.normal(key_coef, (F, RESPONSE_COUNT), jnp.float32) / math.sqrt(F)
    noise = 0.5 * jax.random.normal(key_noise, (OVERALL_LINES, RESPONSE_COUNT), jnp.float32)
    targs = jnp.dot(feats, coefs, precision=lax.Precision.HIGHEST) + noise
    return (feats, targs)


def draw_features(key, part):
    return joint_rows(key)[0]


def draw_response_lines(key, part):
    return joint_rows(key)[1]


def draw_row_counts(key, part):
    units = jax.random.randint(jax.random.fold_in(key, 13), (N_TM,), SHARD // 256, SHARD // 128 + 1)
    return (units * 128).astype(jnp.int32)


def place_ends(values, key, least, top_value):
    dims = values.shape
    spot = [jax.random.randint(jax.random.fold_in(key, axis), (), 0, dims[axis]) for axis in range(len(dims))]
    values = values.at[tuple(spot)].set(least)
    longest = dims.index(max(dims))
    spot[longest] = (spot[longest] + 1) % dims[longest]
    return values.at[tuple(spot)].set(top_value)


def setup_inputs(seed: int = 0) -> dict:
    seeds = jax.random.split(jax.random.key(seed), 5)
    return {
        "features": draw_features(jax.random.fold_in(seeds[4], 71), 0),
        "response_lines": draw_response_lines(jax.random.fold_in(seeds[4], 71), 0),
        "row_counts": draw_row_counts(jax.random.fold_in(seeds[4], 71), 0),
        "ridge_codes": place_ends(jax.random.randint(seeds[3], (N_TM,), 2, 34), jax.random.fold_in(seeds[3], 1), 2, 33).astype(jnp.int32),
    }


def ridge_solve(gram_sum, cross_sum, ridge_value):
    identity = jnp.eye(gram_sum.shape[0], dtype=jnp.float32)
    lower_factor = jnp.linalg.cholesky(gram_sum + ridge_value * identity)
    return jax.scipy.linalg.cho_solve((lower_factor, True), cross_sum)

def reference(features, response_lines, row_counts, ridge_codes):
    regressor_blocks = features.reshape(N_TM, SHARD, F)
    response_partitions = response_lines.reshape(N_TM, SHARD, RESPONSE_COUNT)
    positions = jnp.arange(SHARD, dtype=jnp.int32)
    usable_line_flags = (positions[None, :] < row_counts[:, None]).astype(jnp.float32)

    def shard_terms(packed_pair):
        feat_block, targ_block, valid_block = packed_pair
        weighted = feat_block * valid_block[:, None]
        gram_part = jnp.dot(weighted.T.astype(jnp.float32), feat_block.astype(jnp.float32), precision=lax.Precision.HIGHEST, preferred_element_type=jnp.float32)
        cross_part = jnp.dot(weighted.T.astype(jnp.float32), targ_block.astype(jnp.float32), precision=lax.Precision.HIGHEST, preferred_element_type=jnp.float32)
        return (gram_part, cross_part)
    gram_parts, cross_parts = lax.map(shard_terms, (regressor_blocks, response_partitions, usable_line_flags))
    gram_prefix = jnp.cumsum(gram_parts, axis=0)
    cross_prefix = jnp.cumsum(cross_parts, axis=0)
    seen = jnp.cumsum(row_counts.astype(jnp.float32))
    ridge_values = ridge_codes.astype(jnp.float32) * seen / 16.0

    def solve_single_anchor(packed_pair):
        return ridge_solve(packed_pair[0], packed_pair[1], packed_pair[2])
    weights = lax.map(solve_single_anchor, (gram_prefix, cross_prefix, ridge_values))
    prior_carry = jnp.concatenate([jnp.zeros((1, F, RESPONSE_COUNT), jnp.float32), weights[:-1]], axis=0)
    predicted_result = jnp.einsum('gbr,grd->gbd', regressor_blocks, prior_carry, precision=lax.Precision.HIGHEST) * usable_line_flags[:, :, None]
    residual_list = usable_line_flags[:, :, None] * (response_partitions - predicted_result) ** 2
    partition_mse = jnp.sum(residual_list, axis=(1, 2)) / (row_counts.astype(jnp.float32) * RESPONSE_COUNT)
    return (predicted_result.reshape(OVERALL_LINES, RESPONSE_COUNT).astype(jnp.bfloat16), partition_mse)
```

```python
import functools
import math

import jax
import jax.numpy as jnp
from jax import lax
from jax.experimental import pallas as pl
from jax.experimental.pallas import tpu as pltpu
from jax.sharding import PartitionSpec as P

BF = jnp.bfloat16
F32 = jnp.float32
NN = (((1,), (0,)), ((), ()))
TN = (((0,), (0,)), ((), ()))


def split(value):
    high = value.astype(BF)
    return high, (value - high.astype(F32)).astype(BF)


def dot_bf(a, b, dims):
    return lax.dot_general(a, b, dims, preferred_element_type=F32)


def dot_full(a, b, dims):
    return lax.dot_general(a, b, dims, precision=lax.Precision.HIGHEST, preferred_element_type=F32)


def slots_of(piece, part_rows, sub_parts, core, place, rows):
    part, offset = divmod(rows, part_rows)
    half, sub = divmod(part, sub_parts)
    slot = (half ^ core) * sub_parts + (sub ^ place)
    return pl.ds(pl.multiple_of(slot * part_rows + offset, 8), piece)


def gram_kernel(ids, x_ref, y_ref, o_ref, hh, hl, ch, cl, *, tile, part_rows, sub_parts):
    step = pl.program_id(0)
    f, q = x_ref.shape[1], y_ref.shape[1]
    half = f // 2

    @pl.when(step == 0)
    def _():
        for ref in (hh, hl, ch, cl):
            ref[...] = jnp.zeros_like(ref)

    keep = lax.broadcasted_iota(jnp.int32, (tile, 1), 0) < ids[0] - step * tile
    h, l = split(jnp.where(keep, x_ref[...], 0.0))
    yh, yl = split(jnp.where(keep, y_ref[...], 0.0))
    hh[:, half:] += dot_bf(h, h[:, half:], TN)
    hh[:half, :half] += dot_bf(h[:, :half], h[:, :half], TN)
    hl[...] += dot_bf(h, l, TN)
    ch[...] += dot_bf(h, jnp.concatenate([yh, yl], 1), TN)
    cl[...] += dot_bf(yh, l, TN)

    @pl.when(step == pl.num_programs(0) - 1)
    def _():
        blocks = f // q
        piece = math.gcd(part_rows, q)
        at = 0

        def put(block):
            for r in range(0, q, piece):
                o_ref[slots_of(piece, part_rows, sub_parts, ids[1], ids[2], at + r), :] = block[r : r + piece]

        for i in range(blocks):
            si = slice(i * q, (i + 1) * q)
            for j in range(i, blocks):
                sj = slice(j * q, (j + 1) * q)
                put(hh[si, sj] + (hl[si, sj] + hl[sj, si].T))
                at += q
        for i in range(blocks):
            si = slice(i * q, (i + 1) * q)
            put(ch[si, :q] + (ch[si, q:] + cl[:, si].T))
            at += q


def gram(ids, x, y, parts, sub_parts):
    m, f = x.shape
    q = y.shape[1]
    blocks = f // q
    rows = (blocks * (blocks + 1) // 2 + blocks) * q
    tile = math.gcd(m, 1024)
    return pl.pallas_call(
        functools.partial(gram_kernel, tile=tile, part_rows=rows // parts, sub_parts=sub_parts),
        out_shape=jax.ShapeDtypeStruct((rows, q), F32),
        grid_spec=pltpu.PrefetchScalarGridSpec(
            num_scalar_prefetch=1,
            grid=(m // tile,),
            in_specs=[
                pl.BlockSpec((tile, f), lambda k, ids: (k, 0)),
                pl.BlockSpec((tile, q), lambda k, ids: (k, 0)),
            ],
            out_specs=pl.BlockSpec((rows, q), lambda k, ids: (0, 0)),
            scratch_shapes=[
                pltpu.VMEM((f, f), F32),
                pltpu.VMEM((f, f), F32),
                pltpu.VMEM((f, 2 * q), F32),
                pltpu.VMEM((q, f), F32),
            ],
        ),
        compiler_params=pltpu.CompilerParams(dimension_semantics=("arbitrary",)),
        name="gram",
    )(ids, x, y)


def inverse_factor(groups):
    count, shape = len(groups), groups[0].shape
    lane = lax.broadcasted_iota(jnp.int32, shape, 1)
    sub = lax.broadcasted_iota(jnp.int32, shape, 0)
    spread = lambda v: jnp.broadcast_to(v, shape)
    out = []
    for p in range(count):
        c0 = 8 * p
        here = groups[p]
        cols = [spread(here[:, c0 + b : c0 + b + 1]) for b in range(8)]
        s = [[spread(cols[b][a : a + 1, :]) for b in range(a + 1)] for a in range(8)]
        inside = (lane >= c0) & (lane < c0 + 8)
        open_rows = jnp.where(inside, jnp.where(lane - c0 == sub, 1.0, 0.0), here)
        rows = [spread(open_rows[b : b + 1, :]) for b in range(8)]
        u = [None] * 8
        for b in range(8):
            scale = lax.rsqrt(s[b][b])
            u[b] = rows[b] * scale
            for a in range(b + 1, 8):
                s[a][b] = s[a][b] * scale
            for a in range(b + 1, 8):
                for c in range(b + 1, a + 1):
                    s[a][c] = s[a][c] - s[a][b] * s[c][b]
                rows[a] = rows[a] - s[a][b] * u[b]
            s[b][b] = scale
        v = [None] * 8
        for b in range(7, -1, -1):
            t = u[b]
            for a in range(b + 1, 8):
                t = t - s[a][b] * v[a]
            v[b] = t * s[b][b]
        joined = u[0]
        for a in range(1, 8):
            joined = jnp.where(sub == a, u[a], joined)
        out.append(jnp.where(lane < c0 + 8, joined, 0.0))
        for g in range(p + 1, count):
            t = jnp.where(inside, 0.0, groups[g])
            for b in range(8):
                t = t - spread(groups[g][:, c0 + b : c0 + b + 1]) * v[b]
            groups[g] = t
    return out


def solve_kernel(ridge_ref, ids, *refs, blocks, parts, sub_parts):
    given, w_ref, packed, linv, rows = refs[:parts], refs[parts], refs[parts + 1], refs[parts + 2], refs[parts + 3 :]
    part_rows, q = given[0].shape
    ridge = ridge_ref[0]
    for slot in range(parts):
        half, sub = divmod(slot, sub_parts)
        part = (half ^ ids[1]) * sub_parts + (sub ^ ids[2])
        packed[pl.ds(pl.multiple_of(part * part_rows, 8), part_rows), :] = given[slot][...]
    eye = lax.broadcasted_iota(jnp.int32, (q, q), 0) == lax.broadcasted_iota(jnp.int32, (q, q), 1)
    at = 0
    for i in range(blocks):
        for j in range(i, blocks):
            block = packed[at : at + q, :]
            if i == j:
                block = block + jnp.where(eye, ridge, 0.0)
            rows[i][:, (j - i) * q : (j - i + 1) * q] = block
            at += q
    for i in range(blocks):
        rows[i][:, (blocks - i) * q :] = packed[at : at + q, :]
        at += q
    z = [None] * blocks
    for i in range(blocks):
        inverse = inverse_factor([rows[i][8 * t : 8 * t + 8, :q] for t in range(q // 8)])
        for t in range(q // 8):
            linv[8 * t : 8 * t + 8, :] = inverse[t]
        li = linv[...]
        panel = dot_full(li, rows[i][:, q:], NN)
        for j in range(i + 1, blocks):
            rows[j][...] -= dot_full(panel[:, (j - i - 1) * q : (j - i) * q], panel[:, (j - i - 1) * q :], TN)
        z[i] = dot_full(li, panel, TN)
        for j in range(i):
            z[j] = z[j][:, q:] - dot_full(z[j][:, :q], z[i], NN)
    for i in range(blocks):
        w_ref[i * q : (i + 1) * q, :] = z[i]


def solve(ridge, ids, given, blocks, sub_parts):
    part_rows, q = given[0].shape
    parts = len(given)
    smem, vmem = pl.BlockSpec(memory_space=pltpu.SMEM), pl.BlockSpec(memory_space=pltpu.VMEM)
    return pl.pallas_call(
        functools.partial(solve_kernel, blocks=blocks, parts=parts, sub_parts=sub_parts),
        out_shape=jax.ShapeDtypeStruct((blocks * q, q), F32),
        in_specs=[smem, smem] + [vmem] * parts,
        out_specs=vmem,
        scratch_shapes=[pltpu.VMEM((parts * part_rows, q), F32), pltpu.VMEM((q, q), F32)]
        + [pltpu.VMEM((q, (blocks - i + 1) * q), F32) for i in range(blocks)],
        name="solve",
    )(ridge, ids, *given)


def predict_kernel(ids, x_ref, y_ref, w_ref, o_ref, e_ref, wide, *, tile):
    step = pl.program_id(0)
    q = y_ref.shape[1]

    @pl.when(step == 0)
    def _():
        wide[:, :q], wide[:, q:] = split(w_ref[...])
        e_ref[...] = jnp.zeros_like(e_ref)

    keep = lax.broadcasted_iota(jnp.int32, (tile, 1), 0) < ids[0] - step * tile
    h, l = split(x_ref[...])
    both = dot_bf(h, wide[...], NN)
    value = both[:, :q] + (both[:, q:] + dot_bf(l, wide[:, :q], NN))
    value = jnp.where(keep, value, 0.0)
    o_ref[...] = value.astype(BF)
    gap = jnp.where(keep, y_ref[...] - value, 0.0)
    e_ref[...] += jnp.sum((gap * gap).reshape(tile // 8, 8, q), axis=0)


def predict(ids, x, y, w):
    m, f = x.shape
    q = y.shape[1]
    tile = math.gcd(m, 1024)
    return pl.pallas_call(
        functools.partial(predict_kernel, tile=tile),
        out_shape=(jax.ShapeDtypeStruct((m, q), BF), jax.ShapeDtypeStruct((8, q), F32)),
        grid_spec=pltpu.PrefetchScalarGridSpec(
            num_scalar_prefetch=1,
            grid=(m // tile,),
            in_specs=[
                pl.BlockSpec((tile, f), lambda k, ids: (k, 0)),
                pl.BlockSpec((tile, q), lambda k, ids: (k, 0)),
                pl.BlockSpec((f, q), lambda k, ids: (0, 0)),
            ],
            out_specs=(pl.BlockSpec((tile, q), lambda k, ids: (k, 0)), pl.BlockSpec((8, q), lambda k, ids: (0, 0))),
            scratch_shapes=[pltpu.VMEM((f, 2 * q), BF)],
        ),
        compiler_params=pltpu.CompilerParams(dimension_semantics=("arbitrary",)),
        name="predict",
    )(ids, x, y, w)


def swap(value, axes, size, j):
    return lax.ppermute(value, axes, [(i, i ^ j) for i in range(size)])


def total(values):
    return functools.reduce(jnp.add, values)


def earlier_sums(packed, parts, sub_parts, time_index, row_index, n_time, n_rows):
    part_rows = packed.shape[0] // parts
    core_swap = lambda v: swap(v, "rows", n_rows, 1)
    n_seats = n_rows // 2
    odd = time_index % 2

    def seat_swap(value, j):
        late, seat = divmod(j, n_seats)
        pairs = [
            (t * n_rows + r, (t ^ late) * n_rows + (r ^ (2 * seat))) for t in range(n_time) for r in range(n_rows)
        ]
        return lax.ppermute(value, ("tm", "rows"), pairs)

    half_rows = part_rows * sub_parts
    mine = packed[:half_rows] + core_swap(packed[half_rows:])
    slots = [mine[j * part_rows : (j + 1) * part_rows] for j in range(sub_parts)]
    slots = [slots[0]] + [seat_swap(slots[j], j) for j in range(1, sub_parts)]
    same, other = total(slots[:n_seats]), total(slots[n_seats:])
    both = same + other
    even_part = jnp.where(odd == 1, other, same)
    group = time_index // 2
    before = jnp.zeros_like(both)
    for j in range(1, n_time // 2):
        came = swap(both, "tm", n_time, 2 * j)
        before = before + jnp.where((group ^ j) < group, came, 0.0)
    with_even = before + even_part
    for_same = jnp.where(odd == 1, with_even, before)
    for_other = jnp.where(odd == 1, before, with_even)
    out = [for_same] + [seat_swap(for_same if j < n_seats else for_other, j) for j in range(1, sub_parts)]
    return out + [core_swap(v) for v in out]


def body(features, response_lines, row_counts, ridge_codes, n_time, n_rows):
    m, f = features.shape
    q = response_lines.shape[1]
    time_index, row_index = lax.axis_index("tm"), lax.axis_index("rows")
    counts = row_counts.astype(F32)
    previous = jnp.maximum(time_index - 1, 0)
    seen = jnp.sum(jnp.where(lax.iota(jnp.int32, n_time) <= previous, counts, 0.0))
    ridge = ridge_codes[previous].astype(F32) * seen / 16.0
    sub_parts = n_rows
    parts = 2 * sub_parts
    place = (time_index % 2) * (n_rows // 2) + row_index // 2
    valid = jnp.clip(row_counts[time_index] - row_index * m, 0, m)
    ids = jnp.stack([valid, row_index % 2, place]).astype(jnp.int32)

    packed = gram(ids, features, response_lines, parts, sub_parts)
    given = earlier_sums(packed, parts, sub_parts, time_index, row_index, n_time, n_rows)
    weights = solve(ridge.reshape(1), ids, given, f // q, sub_parts)
    forecast, errors = predict(ids, features, response_lines, weights)
    errors = total([errors] + [swap(errors, "rows", n_rows, j) for j in range(1, n_rows)])
    partition_mse = jnp.sum(errors) / (counts[time_index] * q)
    return forecast, partition_mse.reshape(1)


def solution(mesh):
    return jax.shard_map(
        functools.partial(body, n_time=mesh.shape["tm"], n_rows=mesh.shape["rows"]),
        mesh=mesh,
        in_specs=(P(("tm", "rows"), None), P(("tm", "rows"), None), P(), P()),
        out_specs=(P(("tm", "rows"), None), P("tm")),
        check_vma=False,
    )
```

```python
import functools
import math

import jax
import jax.numpy as jnp
from jax import lax
from jax.experimental import pallas as pl
from jax.experimental.pallas import tpu as pltpu
from jax.sharding import PartitionSpec as P

GRAM_VMEM, SOLVE_VMEM, PREDICT_VMEM = 40 << 20, 12 << 20, 40 << 20
BF = jnp.bfloat16
F32 = jnp.float32
NN = (((1,), (0,)), ((), ()))
TN = (((0,), (0,)), ((), ()))


def in_hbm(value):
    return pltpu.with_memory_space_constraint(value, pltpu.HBM)


def split(value):
    high = value.astype(BF)
    return high, (value - high.astype(F32)).astype(BF)


def dot_bf(a, b, dims):
    return lax.dot_general(a, b, dims, preferred_element_type=F32)


def dot_full(a, b, dims):
    return lax.dot_general(a, b, dims, precision=lax.Precision.HIGHEST, preferred_element_type=F32)


def slot_of(piece, part_rows, sub_parts, place, row):
    part, offset = divmod(row, part_rows)
    half, sub = divmod(part, sub_parts)
    return half, pl.ds(pl.multiple_of((sub ^ place) * part_rows + offset, 8), piece)


def seat(n_rows):
    time_index, row_index = lax.axis_index("tm"), lax.axis_index("rows")
    return row_index % 2, (time_index % 2) * (n_rows // 2) + row_index // 2


def valid_rows(counts, m):
    left = counts[lax.axis_index("tm")] - lax.axis_index("rows") * m
    return jnp.minimum(jnp.maximum(left, 0), m)


def gram_kernel(counts, x_ref, y_ref, mine_ref, send_ref, h_ref, l_ref, hh, hl, ch, cl, *, tile, part_rows, sub_parts):
    step = pl.program_id(0)
    f, q = x_ref.shape[1], y_ref.shape[1]
    half = f // 2

    @pl.when(step == 0)
    def _():
        for ref in (hh, hl, ch, cl):
            ref[...] = jnp.zeros_like(ref)

    m = tile * pl.num_programs(0)
    keep = lax.broadcasted_iota(jnp.int32, (tile, 1), 0) < valid_rows(counts, m) - step * tile
    h, l = split(jnp.where(keep, x_ref[...], 0.0))
    yh, yl = split(jnp.where(keep, y_ref[...], 0.0))
    h_ref[...] = h
    l_ref[...] = l
    hh[:, half:] += dot_bf(h, h[:, half:], TN)
    hh[:half, :half] += dot_bf(h[:, :half], h[:, :half], TN)
    hl[...] += dot_bf(h, l, TN)
    ch[...] += dot_bf(h, jnp.concatenate([yh, yl], 1), TN)
    cl[...] += dot_bf(yh, l, TN)

    @pl.when(step == pl.num_programs(0) - 1)
    def _():
        blocks = f // q
        piece = math.gcd(part_rows, q)
        at = 0
        core, place = seat(sub_parts)

        def put(block):
            for r in range(0, q, piece):
                half, where = slot_of(piece, part_rows, sub_parts, place, at + r)

                @pl.when(core == half)
                def _(r=r, where=where):
                    mine_ref[where, :] = block[r : r + piece]

                @pl.when(core != half)
                def _(r=r, where=where):
                    send_ref[where, :] = block[r : r + piece]

        for i in range(blocks):
            si = slice(i * q, (i + 1) * q)
            for j in range(i, blocks):
                sj = slice(j * q, (j + 1) * q)
                put(hh[si, sj] + (hl[si, sj] + hl[sj, si].T))
                at += q
        for i in range(blocks):
            si = slice(i * q, (i + 1) * q)
            put(ch[si, :q] + (ch[si, q:] + cl[:, si].T))
            at += q


def gram(counts, x, y, sub_parts):
    m, f = x.shape
    q = y.shape[1]
    blocks = f // q
    rows = (blocks * (blocks + 1) // 2 + blocks) * q
    tile = math.gcd(m, 1024)
    half = pl.BlockSpec((rows // 2, q), lambda k, ids: (0, 0))
    wide = pl.BlockSpec((tile, f), lambda k, ids: (k, 0))
    return pl.pallas_call(
        functools.partial(gram_kernel, tile=tile, part_rows=rows // (2 * sub_parts), sub_parts=sub_parts),
        out_shape=[jax.ShapeDtypeStruct((rows // 2, q), F32)] * 2 + [pltpu.HBM((m, f), BF)] * 2,
        grid_spec=pltpu.PrefetchScalarGridSpec(
            num_scalar_prefetch=1,
            grid=(m // tile,),
            in_specs=[
                wide,
                pl.BlockSpec((tile, q), lambda k, ids: (k, 0)),
            ],
            out_specs=[half, half, wide, wide],
            scratch_shapes=[
                pltpu.VMEM((f, f), F32),
                pltpu.VMEM((f, f), F32),
                pltpu.VMEM((f, 2 * q), F32),
                pltpu.VMEM((q, f), F32),
            ],
        ),
        compiler_params=pltpu.CompilerParams(dimension_semantics=("arbitrary",), vmem_limit_bytes=GRAM_VMEM),
        name="gram",
    )(counts, in_hbm(x), in_hbm(y))


def inverse_factor(groups):
    count, shape = len(groups), groups[0].shape
    lane = lax.broadcasted_iota(jnp.int32, shape, 1)
    sub = lax.broadcasted_iota(jnp.int32, shape, 0)
    spread = lambda v: jnp.broadcast_to(v, shape)
    out = []
    for p in range(count):
        c0 = 8 * p
        here = groups[p]
        cols = [spread(here[:, c0 + b : c0 + b + 1]) for b in range(8)]
        s = [[spread(cols[b][a : a + 1, :]) for b in range(a + 1)] for a in range(8)]
        inside = (lane >= c0) & (lane < c0 + 8)
        open_rows = jnp.where(inside, jnp.where(lane - c0 == sub, 1.0, 0.0), here)
        rows = [spread(open_rows[b : b + 1, :]) for b in range(8)]
        u = [None] * 8
        for b in range(8):
            scale = lax.rsqrt(s[b][b])
            u[b] = rows[b] * scale
            for a in range(b + 1, 8):
                s[a][b] = s[a][b] * scale
            for a in range(b + 1, 8):
                for c in range(b + 1, a + 1):
                    s[a][c] = s[a][c] - s[a][b] * s[c][b]
                rows[a] = rows[a] - s[a][b] * u[b]
            s[b][b] = scale
        v = [None] * 8
        for b in range(7, -1, -1):
            t = u[b]
            for a in range(b + 1, 8):
                t = t - s[a][b] * v[a]
            v[b] = t * s[b][b]
        joined = u[0]
        for a in range(1, 8):
            joined = jnp.where(sub == a, u[a], joined)
        out.append(jnp.where(lane < c0 + 8, joined, 0.0))
        for g in range(p + 1, count):
            t = jnp.where(inside, 0.0, groups[g])
            for b in range(8):
                t = t - spread(groups[g][:, c0 + b : c0 + b + 1]) * v[b]
            groups[g] = t
    return out


def solve_kernel(counts, codes, *refs, blocks, parts, sub_parts):
    given, w_ref, packed, linv, rows = refs[:parts], refs[parts], refs[parts + 1], refs[parts + 2], refs[parts + 3 :]
    part_rows, q = given[0].shape
    previous = jnp.maximum(lax.axis_index("tm") - 1, 0)
    seen = lax.fori_loop(0, previous + 1, lambda k, t: t + counts[k], jnp.int32(0))
    ridge = codes[previous].astype(F32) * seen.astype(F32) / 16.0
    core, place = seat(sub_parts)
    for slot in range(parts):
        half, sub = divmod(slot, sub_parts)
        part = (half ^ core) * sub_parts + (sub ^ place)
        packed[pl.ds(pl.multiple_of(part * part_rows, 8), part_rows), :] = given[slot][...]
    eye = lax.broadcasted_iota(jnp.int32, (q, q), 0) == lax.broadcasted_iota(jnp.int32, (q, q), 1)
    at = 0
    for i in range(blocks):
        for j in range(i, blocks):
            block = packed[at : at + q, :]
            if i == j:
                block = block + jnp.where(eye, ridge, 0.0)
            rows[i][:, (j - i) * q : (j - i + 1) * q] = block
            at += q
    for i in range(blocks):
        rows[i][:, (blocks - i) * q :] = packed[at : at + q, :]
        at += q
    z = [None] * blocks
    for i in range(blocks):
        inverse = inverse_factor([rows[i][8 * t : 8 * t + 8, :q] for t in range(q // 8)])
        for t in range(q // 8):
            linv[8 * t : 8 * t + 8, :] = inverse[t]
        li = linv[...]
        panel = dot_full(li, rows[i][:, q:], NN)
        for j in range(i + 1, blocks):
            rows[j][...] -= dot_full(panel[:, (j - i - 1) * q : (j - i) * q], panel[:, (j - i - 1) * q :], TN)
        z[i] = dot_full(li, panel, TN)
        for j in range(i):
            z[j] = z[j][:, q:] - dot_full(z[j][:, :q], z[i], NN)
    for i in range(blocks):
        w_ref[i * q : (i + 1) * q, :] = z[i]


def solve(counts, codes, given, blocks, sub_parts):
    part_rows, q = given[0].shape
    parts = len(given)
    smem, vmem = pl.BlockSpec(memory_space=pltpu.SMEM), pl.BlockSpec(memory_space=pltpu.VMEM)
    return pl.pallas_call(
        functools.partial(solve_kernel, blocks=blocks, parts=parts, sub_parts=sub_parts),
        out_shape=jax.ShapeDtypeStruct((blocks * q, q), F32),
        in_specs=[smem, smem] + [vmem] * parts,
        out_specs=vmem,
        scratch_shapes=[pltpu.VMEM((parts * part_rows, q), F32), pltpu.VMEM((q, q), F32)]
        + [pltpu.VMEM((q, (blocks - i + 1) * q), F32) for i in range(blocks)],
        compiler_params=pltpu.CompilerParams(vmem_limit_bytes=SOLVE_VMEM),
        name="solve",
    )(counts, codes, *given)


def predict_kernel(counts, h_ref, l_ref, y_ref, w_ref, o_ref, e_ref, wide, acc, *, tile):
    step = pl.program_id(0)
    q = y_ref.shape[1]

    @pl.when(step == 0)
    def _():
        wide[:, :q], wide[:, q:] = split(w_ref[...])
        acc[...] = jnp.zeros_like(acc)

    m = tile * pl.num_programs(0)
    keep = lax.broadcasted_iota(jnp.int32, (tile, 1), 0) < valid_rows(counts, m) - step * tile
    both = dot_bf(h_ref[...], wide[...], NN)
    value = both[:, :q] + (both[:, q:] + dot_bf(l_ref[...], wide[:, :q], NN))
    value = jnp.where(keep, value, 0.0)
    o_ref[...] = value.astype(BF)
    gap = jnp.where(keep, y_ref[...] - value, 0.0)
    acc[...] += jnp.sum((gap * gap).reshape(tile // 8, 8, q), axis=0)

    @pl.when(step == pl.num_programs(0) - 1)
    def _():
        share = counts[lax.axis_index("tm")].astype(F32) * q
        e_ref[...] = jnp.sum(jnp.sum(acc[...], axis=1, keepdims=True), axis=0, keepdims=True) / share


def predict(counts, h, l, y, w):
    m, f = h.shape
    held = pl.BlockSpec(memory_space=pltpu.VMEM)
    q = y.shape[1]
    tile = math.gcd(m, 1024)
    return pl.pallas_call(
        functools.partial(predict_kernel, tile=tile),
        out_shape=(jax.ShapeDtypeStruct((m, q), BF), jax.ShapeDtypeStruct((1, 1), F32)),
        grid_spec=pltpu.PrefetchScalarGridSpec(
            num_scalar_prefetch=1,
            grid=(m // tile,),
            in_specs=[
                pl.BlockSpec((tile, f), lambda k, ids: (k, 0)),
                pl.BlockSpec((tile, f), lambda k, ids: (k, 0)),
                pl.BlockSpec((tile, q), lambda k, ids: (k, 0)),
                held,
            ],
            out_specs=(pl.BlockSpec((tile, q), lambda k, ids: (k, 0)), held),
            scratch_shapes=[pltpu.VMEM((f, 2 * q), BF), pltpu.VMEM((8, q), F32)],
        ),
        compiler_params=pltpu.CompilerParams(dimension_semantics=("arbitrary",), vmem_limit_bytes=PREDICT_VMEM),
        name="predict",
    )(counts, in_hbm(h), in_hbm(l), in_hbm(y), w)


def swap(value, axes, size, j):
    return lax.ppermute(value, axes, [(i, i ^ j) for i in range(size)])


def total(values):
    return functools.reduce(jnp.add, values)


def earlier_sums(mine, sent, n_time, n_rows):
    sub_parts = n_rows
    part_rows = mine.shape[0] // sub_parts
    core_swap = lambda v: swap(v, "rows", n_rows, 1)
    n_seats = n_rows // 2
    time_index = lax.axis_index("tm")
    odd = time_index % 2

    def seat_swap(value, j):
        late, seat = divmod(j, n_seats)
        pairs = [
            (t * n_rows + r, (t ^ late) * n_rows + (r ^ (2 * seat))) for t in range(n_time) for r in range(n_rows)
        ]
        return lax.ppermute(value, ("tm", "rows"), pairs)

    mine = mine + core_swap(sent)
    slots = [mine[j * part_rows : (j + 1) * part_rows] for j in range(sub_parts)]
    slots = [slots[0]] + [seat_swap(slots[j], j) for j in range(1, sub_parts)]
    same, other = total(slots[:n_seats]), total(slots[n_seats:])
    both = same + other
    even_part = jnp.where(odd == 1, other, same)
    group = time_index // 2
    before = jnp.zeros_like(both)
    for j in range(1, n_time // 2):
        came = swap(both, "tm", n_time, 2 * j)
        before = before + jnp.where((group ^ j) < group, came, 0.0)
    with_even = before + even_part
    for_same = jnp.where(odd == 1, with_even, before)
    for_other = jnp.where(odd == 1, before, with_even)
    out = [for_same] + [seat_swap(for_same if j < n_seats else for_other, j) for j in range(1, sub_parts)]
    return out + [core_swap(v) for v in out]


def body(features, response_lines, row_counts, ridge_codes, n_time, n_rows):
    f, q = features.shape[1], response_lines.shape[1]
    mine, sent, high, low = gram(row_counts, features, response_lines, n_rows)
    given = earlier_sums(mine, sent, n_time, n_rows)
    weights = solve(row_counts, ridge_codes, given, f // q, n_rows)
    forecast, error = predict(row_counts, high, low, response_lines, weights)
    partition_mse = total([error] + [swap(error, "rows", n_rows, j) for j in range(1, n_rows)])
    return forecast, partition_mse.reshape(1)


def solution(mesh):
    return jax.shard_map(
        functools.partial(body, n_time=mesh.shape["tm"], n_rows=mesh.shape["rows"]),
        mesh=mesh,
        in_specs=(P(("tm", "rows"), None), P(("tm", "rows"), None), P(), P()),
        out_specs=(P(("tm", "rows"), None), P("tm")),
        check_vma=False,
    )
```

```python
import functools
import math

import jax
import jax.numpy as jnp
from jax import lax
from jax.experimental import pallas as pl
from jax.experimental.pallas import tpu as pltpu
from jax.sharding import PartitionSpec as P

GRAM_VMEM, FIT_VMEM = 40 << 20, 48 << 20
BF = jnp.bfloat16
F32 = jnp.float32
NN = (((1,), (0,)), ((), ()))
TN = (((0,), (0,)), ((), ()))


def in_hbm(value):
    return pltpu.with_memory_space_constraint(value, pltpu.HBM)


def split(value):
    high = value.astype(BF)
    return high, (value - high.astype(F32)).astype(BF)


def dot_bf(a, b, dims):
    return lax.dot_general(a, b, dims, preferred_element_type=F32)


def dot_full(a, b, dims):
    return lax.dot_general(a, b, dims, precision=lax.Precision.HIGHEST, preferred_element_type=F32)


def slot_of(piece, part_rows, sub_parts, place, row):
    part, offset = divmod(row, part_rows)
    half, sub = divmod(part, sub_parts)
    return half, pl.ds(pl.multiple_of((sub ^ place) * part_rows + offset, 8), piece)


def seat(n_rows):
    time_index, row_index = lax.axis_index("tm"), lax.axis_index("rows")
    return row_index % 2, (time_index % 2) * (n_rows // 2) + row_index // 2


def valid_rows(counts, m):
    left = counts[lax.axis_index("tm")] - lax.axis_index("rows") * m
    return jnp.minimum(jnp.maximum(left, 0), m)


def gram_kernel(counts, x_ref, y_ref, mine_ref, send_ref, hh, hl, ch, cl, *, tile, part_rows, sub_parts):
    step = pl.program_id(0)
    f, q = x_ref.shape[1], y_ref.shape[1]
    half = f // 2

    @pl.when(step == 0)
    def _():
        for ref in (hh, hl, ch, cl):
            ref[...] = jnp.zeros_like(ref)

    m = tile * pl.num_programs(0)
    keep = lax.broadcasted_iota(jnp.int32, (tile, 1), 0) < valid_rows(counts, m) - step * tile
    h, l = split(jnp.where(keep, x_ref[...], 0.0))
    yh, yl = split(jnp.where(keep, y_ref[...], 0.0))
    hh[:, half:] += dot_bf(h, h[:, half:], TN)
    hh[:half, :half] += dot_bf(h[:, :half], h[:, :half], TN)
    hl[...] += dot_bf(h, l, TN)
    ch[...] += dot_bf(h, jnp.concatenate([yh, yl], 1), TN)
    cl[...] += dot_bf(yh, l, TN)

    @pl.when(step == pl.num_programs(0) - 1)
    def _():
        blocks = f // q
        piece = math.gcd(part_rows, q)
        at = 0
        core, place = seat(sub_parts)

        def put(block):
            for r in range(0, q, piece):
                half, where = slot_of(piece, part_rows, sub_parts, place, at + r)

                @pl.when(core == half)
                def _(r=r, where=where):
                    mine_ref[where, :] = block[r : r + piece]

                @pl.when(core != half)
                def _(r=r, where=where):
                    send_ref[where, :] = block[r : r + piece]

        for i in range(blocks):
            si = slice(i * q, (i + 1) * q)
            for j in range(i, blocks):
                sj = slice(j * q, (j + 1) * q)
                put(hh[si, sj] + (hl[si, sj] + hl[sj, si].T))
                at += q
        for i in range(blocks):
            si = slice(i * q, (i + 1) * q)
            put(ch[si, :q] + (ch[si, q:] + cl[:, si].T))
            at += q


def gram(counts, x, y, sub_parts):
    m, f = x.shape
    q = y.shape[1]
    blocks = f // q
    rows = (blocks * (blocks + 1) // 2 + blocks) * q
    tile = math.gcd(m, 1024)
    half = pl.BlockSpec((rows // 2, q), lambda k, ids: (0, 0))
    return pl.pallas_call(
        functools.partial(gram_kernel, tile=tile, part_rows=rows // (2 * sub_parts), sub_parts=sub_parts),
        out_shape=[jax.ShapeDtypeStruct((rows // 2, q), F32)] * 2,
        grid_spec=pltpu.PrefetchScalarGridSpec(
            num_scalar_prefetch=1,
            grid=(m // tile,),
            in_specs=[
                pl.BlockSpec((tile, f), lambda k, ids: (k, 0)),
                pl.BlockSpec((tile, q), lambda k, ids: (k, 0)),
            ],
            out_specs=[half, half],
            scratch_shapes=[
                pltpu.VMEM((f, f), F32),
                pltpu.VMEM((f, f), F32),
                pltpu.VMEM((f, 2 * q), F32),
                pltpu.VMEM((q, f), F32),
            ],
        ),
        compiler_params=pltpu.CompilerParams(dimension_semantics=("arbitrary",), vmem_limit_bytes=GRAM_VMEM),
        name="gram",
    )(counts, in_hbm(x), in_hbm(y))


def inverse_factor(groups):
    count, shape = len(groups), groups[0].shape
    lane = lax.broadcasted_iota(jnp.int32, shape, 1)
    sub = lax.broadcasted_iota(jnp.int32, shape, 0)
    spread = lambda v: jnp.broadcast_to(v, shape)
    out = []
    for p in range(count):
        c0 = 8 * p
        here = groups[p]
        cols = [spread(here[:, c0 + b : c0 + b + 1]) for b in range(8)]
        s = [[spread(cols[b][a : a + 1, :]) for b in range(a + 1)] for a in range(8)]
        inside = (lane >= c0) & (lane < c0 + 8)
        open_rows = jnp.where(inside, jnp.where(lane - c0 == sub, 1.0, 0.0), here)
        rows = [spread(open_rows[b : b + 1, :]) for b in range(8)]
        u = [None] * 8
        for b in range(8):
            scale = lax.rsqrt(s[b][b])
            u[b] = rows[b] * scale
            for a in range(b + 1, 8):
                s[a][b] = s[a][b] * scale
            for a in range(b + 1, 8):
                for c in range(b + 1, a + 1):
                    s[a][c] = s[a][c] - s[a][b] * s[c][b]
                rows[a] = rows[a] - s[a][b] * u[b]
            s[b][b] = scale
        v = [None] * 8
        for b in range(7, -1, -1):
            t = u[b]
            for a in range(b + 1, 8):
                t = t - s[a][b] * v[a]
            v[b] = t * s[b][b]
        joined = u[0]
        for a in range(1, 8):
            joined = jnp.where(sub == a, u[a], joined)
        out.append(jnp.where(lane < c0 + 8, joined, 0.0))
        for g in range(p + 1, count):
            t = jnp.where(inside, 0.0, groups[g])
            for b in range(8):
                t = t - spread(groups[g][:, c0 + b : c0 + b + 1]) * v[b]
            groups[g] = t
    return out


def solve_into(z, counts, codes, given, packed, linv, rows):
    blocks, parts = len(rows), len(given)
    sub_parts = parts // 2
    part_rows, q = given[0].shape
    previous = jnp.maximum(lax.axis_index("tm") - 1, 0)
    seen = lax.fori_loop(0, previous + 1, lambda k, t: t + counts[k], jnp.int32(0))
    ridge = codes[previous].astype(F32) * seen.astype(F32) / 16.0
    core, place = seat(sub_parts)
    for slot in range(parts):
        half, sub = divmod(slot, sub_parts)
        part = (half ^ core) * sub_parts + (sub ^ place)
        packed[pl.ds(pl.multiple_of(part * part_rows, 8), part_rows), :] = given[slot][...]
    eye = lax.broadcasted_iota(jnp.int32, (q, q), 0) == lax.broadcasted_iota(jnp.int32, (q, q), 1)
    at = 0
    for i in range(blocks):
        for j in range(i, blocks):
            block = packed[at : at + q, :]
            if i == j:
                block = block + jnp.where(eye, ridge, 0.0)
            rows[i][:, (j - i) * q : (j - i + 1) * q] = block
            at += q
    for i in range(blocks):
        rows[i][:, (blocks - i) * q :] = packed[at : at + q, :]
        at += q
    for i in range(blocks):
        inverse = inverse_factor([rows[i][8 * t : 8 * t + 8, :q] for t in range(q // 8)])
        for t in range(q // 8):
            linv[8 * t : 8 * t + 8, :] = inverse[t]
        li = linv[...]
        panel = dot_full(li, rows[i][:, q:], NN)
        for j in range(i + 1, blocks):
            rows[j][...] -= dot_full(panel[:, (j - i - 1) * q : (j - i) * q], panel[:, (j - i - 1) * q :], TN)
        z.append(dot_full(li, panel, TN))
        for j in range(i):
            z[j] = z[j][:, q:] - dot_full(z[j][:, :q], z[i], NN)


def fit_kernel(counts, codes, x_hbm, y_hbm, *refs, parts, blocks, tile):
    given, o_hbm, e_ref = refs[:parts], refs[parts], refs[parts + 1]
    x, y, o, wide, acc, packed, linv, sems = refs[parts + 2 : parts + 10]
    rows = refs[parts + 10 :]
    m, q = y.shape
    tiles = m // tile

    def moves(k):
        now = pl.ds(pl.multiple_of(k * tile, tile), tile)
        return (
            pltpu.make_async_copy(x_hbm.at[now, :], x.at[now, :], sems.at[0, k]),
            pltpu.make_async_copy(y_hbm.at[now, :], y.at[now, :], sems.at[1, k]),
            pltpu.make_async_copy(o.at[now, :], o_hbm.at[now, :], sems.at[2, k]),
        )

    for k in range(tiles):
        for copy in moves(k)[:2]:
            copy.start()
    z = []
    solve_into(z, counts, codes, given, packed, linv, rows)
    for i in range(blocks):
        here = slice(i * q, (i + 1) * q)
        wide[here, :q], wide[here, q:] = split(z[i])
    acc[...] = jnp.zeros_like(acc)
    valid = valid_rows(counts, m)

    @pl.loop(0, tiles)
    def _(k):
        x_in, y_in, out = moves(k)
        x_in.wait()
        y_in.wait()
        now = pl.ds(pl.multiple_of(k * tile, tile), tile)
        keep = lax.broadcasted_iota(jnp.int32, (tile, 1), 0) < valid - k * tile
        h, l = split(x[now, :])
        both = dot_bf(h, wide[...], NN)
        value = both[:, :q] + (both[:, q:] + dot_bf(l, wide[:, :q], NN))
        value = jnp.where(keep, value, 0.0)
        o[now, :] = value.astype(BF)
        out.start()
        gap = jnp.where(keep, y[now, :] - value, 0.0)
        acc[...] += jnp.sum((gap * gap).reshape(tile // 8, 8, q), axis=0)

    share = counts[lax.axis_index("tm")].astype(F32) * q
    e_ref[...] = jnp.broadcast_to(jnp.sum(acc[...]) / share, (1, q))

    @pl.loop(0, tiles)
    def _(k):
        moves(k)[2].wait()


def fit(counts, codes, x, y, given):
    m, f = x.shape
    q = y.shape[1]
    blocks, parts, tile = f // q, len(given), math.gcd(m, 1024)
    smem, vmem, hbm = (pl.BlockSpec(memory_space=s) for s in (pltpu.SMEM, pltpu.VMEM, pl.ANY))
    return pl.pallas_call(
        functools.partial(fit_kernel, blocks=blocks, parts=parts, tile=tile),
        out_shape=(pltpu.HBM((m, q), BF), jax.ShapeDtypeStruct((1, q), F32)),
        in_specs=[smem, smem, hbm, hbm] + [vmem] * parts,
        out_specs=(hbm, vmem),
        scratch_shapes=[
            pltpu.VMEM((m, f), F32),
            pltpu.VMEM((m, q), F32),
            pltpu.VMEM((m, q), BF),
            pltpu.VMEM((f, 2 * q), BF),
            pltpu.VMEM((8, q), F32),
            pltpu.VMEM((parts * given[0].shape[0], q), F32),
            pltpu.VMEM((q, q), F32),
            pltpu.SemaphoreType.DMA((3, m // tile)),
        ]
        + [pltpu.VMEM((q, (blocks - i + 1) * q), F32) for i in range(blocks)],
        compiler_params=pltpu.CompilerParams(vmem_limit_bytes=FIT_VMEM),
        name="fit",
    )(counts, codes, in_hbm(x), in_hbm(y), *given)


def swap(value, axes, size, j):
    return lax.ppermute(value, axes, [(i, i ^ j) for i in range(size)])


def total(values):
    return functools.reduce(jnp.add, values)


def earlier_sums(mine, sent, n_time, n_rows):
    sub_parts = n_rows
    part_rows = mine.shape[0] // sub_parts
    core_swap = lambda v: swap(v, "rows", n_rows, 1)
    n_seats = n_rows // 2
    time_index = lax.axis_index("tm")
    odd = time_index % 2

    def seat_swap(value, j):
        late, seat = divmod(j, n_seats)
        pairs = [
            (t * n_rows + r, (t ^ late) * n_rows + (r ^ (2 * seat))) for t in range(n_time) for r in range(n_rows)
        ]
        return lax.ppermute(value, ("tm", "rows"), pairs)

    mine = mine + core_swap(sent)
    slots = [mine[j * part_rows : (j + 1) * part_rows] for j in range(sub_parts)]
    slots = [slots[0]] + [seat_swap(slots[j], j) for j in range(1, sub_parts)]
    same, other = total(slots[:n_seats]), total(slots[n_seats:])
    both = same + other
    even_part = jnp.where(odd == 1, other, same)
    group = time_index // 2
    before = jnp.zeros_like(both)
    for j in range(1, n_time // 2):
        came = swap(both, "tm", n_time, 2 * j)
        before = before + jnp.where((group ^ j) < group, came, 0.0)
    with_even = before + even_part
    for_same = jnp.where(odd == 1, with_even, before)
    for_other = jnp.where(odd == 1, before, with_even)
    out = [for_same] + [seat_swap(for_same if j < n_seats else for_other, j) for j in range(1, sub_parts)]
    return out + [core_swap(v) for v in out]


def body(features, response_lines, row_counts, ridge_codes, n_time, n_rows):
    mine, sent = gram(row_counts, features, response_lines, n_rows)
    given = earlier_sums(mine, sent, n_time, n_rows)
    forecast, error = fit(row_counts, ridge_codes, features, response_lines, given)
    partition_mse = total([error] + [swap(error, "rows", n_rows, j) for j in range(1, n_rows)])
    return forecast, partition_mse[0, :1]


def solution(mesh):
    return jax.shard_map(
        functools.partial(body, n_time=mesh.shape["tm"], n_rows=mesh.shape["rows"]),
        mesh=mesh,
        in_specs=(P(("tm", "rows"), None), P(("tm", "rows"), None), P(), P()),
        out_specs=(P(("tm", "rows"), None), P("tm")),
        check_vma=False,
    )
```

```python
import functools
import math

import jax
import jax.numpy as jnp
from jax import lax
from jax.experimental import pallas as pl
from jax.experimental.pallas import tpu as pltpu
from jax.sharding import PartitionSpec as P

GRAM_VMEM, FIT_VMEM = 40 << 20, 48 << 20
BF = jnp.bfloat16
F32 = jnp.float32
NN = (((1,), (0,)), ((), ()))
TN = (((0,), (0,)), ((), ()))


def in_hbm(value):
    return pltpu.with_memory_space_constraint(value, pltpu.HBM)


def split(value):
    high = value.astype(BF)
    return high, (value - high.astype(F32)).astype(BF)


def dot_bf(a, b, dims):
    return lax.dot_general(a, b, dims, preferred_element_type=F32)


def slot_of(piece, part_rows, sub_parts, place, row):
    part, offset = divmod(row, part_rows)
    half, sub = divmod(part, sub_parts)
    return half, pl.ds(pl.multiple_of((sub ^ place) * part_rows + offset, 8), piece)


def seat(n_rows):
    time_index, row_index = lax.axis_index("tm"), lax.axis_index("rows")
    return row_index % 2, (time_index % 2) * (n_rows // 2) + row_index // 2


def valid_rows(counts, m):
    left = counts[lax.axis_index("tm")] - lax.axis_index("rows") * m
    return jnp.minimum(jnp.maximum(left, 0), m)


def gram_kernel(counts, x_ref, y_ref, mine_ref, send_ref, hh, hl, ch, cl, *, tile, part_rows, sub_parts):
    step = pl.program_id(0)
    f, q = x_ref.shape[1], y_ref.shape[1]
    half = f // 2

    @pl.when(step == 0)
    def _():
        for ref in (hh, hl, ch, cl):
            ref[...] = jnp.zeros_like(ref)

    m = tile * pl.num_programs(0)
    keep = lax.broadcasted_iota(jnp.int32, (tile, 1), 0) < valid_rows(counts, m) - step * tile
    h, l = split(jnp.where(keep, x_ref[...], 0.0))
    yh, yl = split(jnp.where(keep, y_ref[...], 0.0))
    hh[:, half:] += dot_bf(h, h[:, half:], TN)
    hh[:half, :half] += dot_bf(h[:, :half], h[:, :half], TN)
    hl[...] += dot_bf(h, l, TN)
    ch[...] += dot_bf(h, jnp.concatenate([yh, yl], 1), TN)
    cl[...] += dot_bf(yh, l, TN)

    @pl.when(step == pl.num_programs(0) - 1)
    def _():
        blocks = f // q
        piece = math.gcd(part_rows, q)
        at = 0
        core, place = seat(sub_parts)

        def put(block):
            for r in range(0, q, piece):
                half, where = slot_of(piece, part_rows, sub_parts, place, at + r)

                @pl.when(core == half)
                def _(r=r, where=where):
                    mine_ref[where, :] = block[r : r + piece]

                @pl.when(core != half)
                def _(r=r, where=where):
                    send_ref[where, :] = block[r : r + piece]

        for i in range(blocks):
            si = slice(i * q, (i + 1) * q)
            for j in range(i, blocks):
                sj = slice(j * q, (j + 1) * q)
                put(hh[si, sj] + (hl[si, sj] + hl[sj, si].T))
                at += q
        for i in range(blocks):
            si = slice(i * q, (i + 1) * q)
            put(ch[si, :q] + (ch[si, q:] + cl[:, si].T))
            at += q


def gram(counts, x, y, sub_parts):
    m, f = x.shape
    q = y.shape[1]
    blocks = f // q
    rows = (blocks * (blocks + 1) // 2 + blocks) * q
    tile = math.gcd(m, 1024)
    half = pl.BlockSpec((rows // 2, q), lambda k, ids: (0, 0))
    return pl.pallas_call(
        functools.partial(gram_kernel, tile=tile, part_rows=rows // (2 * sub_parts), sub_parts=sub_parts),
        out_shape=[jax.ShapeDtypeStruct((rows // 2, q), F32)] * 2,
        grid_spec=pltpu.PrefetchScalarGridSpec(
            num_scalar_prefetch=1,
            grid=(m // tile,),
            in_specs=[
                pl.BlockSpec((tile, f), lambda k, ids: (k, 0)),
                pl.BlockSpec((tile, q), lambda k, ids: (k, 0)),
            ],
            out_specs=[half, half],
            scratch_shapes=[
                pltpu.VMEM((f, f), F32),
                pltpu.VMEM((f, f), F32),
                pltpu.VMEM((f, 2 * q), F32),
                pltpu.VMEM((q, f), F32),
            ],
        ),
        compiler_params=pltpu.CompilerParams(dimension_semantics=("arbitrary",), vmem_limit_bytes=GRAM_VMEM),
        name="gram",
    )(counts, in_hbm(x), in_hbm(y))


def inverse_factor(groups, span=4):
    count, shape = len(groups), groups[0].shape
    lane = lax.broadcasted_iota(jnp.int32, shape, 1)
    sub = lax.broadcasted_iota(jnp.int32, shape, 0)
    spread = lambda v: jnp.broadcast_to(v, shape)
    out = []
    for k in range(0, count, span):
        c0, width = 8 * k, 8 * span
        inside = (lane >= c0) & (lane < c0 + width)
        col = [[spread(groups[k + g][:, c0 + c : c0 + c + 1]) for c in range(8 * g + 8)] for g in range(span)]
        col[0][0] = col[0][0] + 0.0
        rows = [
            jnp.where(inside, jnp.where(lane - c0 - 8 * g == sub, 1.0, 0.0), groups[k + g]) for g in range(span)
        ]
        for b in range(width):
            g0, r = divmod(b, 8)
            scale = lax.rsqrt(spread(col[g0][b][r : r + 1, :]))
            factor = {g: col[g][b] * scale for g in range(g0, span)}
            for c in range(b + 1, width):
                gc, rc = divmod(c, 8)
                other = spread(factor[gc][rc : rc + 1, :])
                for g in range(gc, span):
                    col[g][c] = col[g][c] - factor[g] * other
            u = spread(rows[g0][r : r + 1, :]) * scale
            rows[g0] = jnp.where(sub == r, u, rows[g0] - jnp.where(sub > r, factor[g0], 0.0) * u)
            for g in range(g0 + 1, span):
                rows[g] = rows[g] - factor[g] * u
        out += [jnp.where(lane < c0 + width, v, 0.0) for v in rows]
        if k + span < count:
            h, l = split(jnp.concatenate(rows, 0))
            change = dot_bf(jnp.concatenate([h, h, l], 0), jnp.concatenate([h, l, h], 0), TN)
            for g in range(k + span, count):
                groups[g] = jnp.where(inside, 0.0, groups[g]) - change[8 * g : 8 * g + 8]
    return out


def split3(value):
    high = value.astype(BF)
    rest = value - high.astype(F32)
    return (high,) + split(rest)


def dot_six(a, b, dims):
    left = jnp.concatenate([a[i] for i in (0, 0, 1, 0, 2, 1)], dims[0][0][0])
    right = jnp.concatenate([b[i] for i in (0, 1, 0, 2, 0, 1)], dims[0][1][0])
    return dot_bf(left, right, dims)


def solve_into(z, counts, codes, given, packed, linv, tiles):
    parts = len(given)
    sub_parts = parts // 2
    part_rows, q = given[0].shape
    blocks = next(n for n in range(1, len(tiles) + 1) if n * (n + 1) // 2 + n == len(tiles))
    previous = jnp.maximum(lax.axis_index("tm") - 1, 0)
    seen = lax.fori_loop(0, previous + 1, lambda k, t: t + counts[k], jnp.int32(0))
    ridge = codes[previous].astype(F32) * seen.astype(F32) / 16.0
    core, place = seat(sub_parts)
    for slot in range(parts):
        half, sub = divmod(slot, sub_parts)
        part = (half ^ core) * sub_parts + (sub ^ place)
        packed[pl.ds(pl.multiple_of(part * part_rows, 8), part_rows), :] = given[slot][...]
    eye = lax.broadcasted_iota(jnp.int32, (q, q), 0) == lax.broadcasted_iota(jnp.int32, (q, q), 1)
    order = [(i, j) for i in range(blocks) for j in range(i, blocks)] + [(i, blocks) for i in range(blocks)]
    a = {}
    for n, (i, j) in enumerate(order):
        block = packed[n * q : (n + 1) * q, :]
        a[i, j] = tiles[n]
        a[i, j][...] = block + jnp.where(eye, ridge, 0.0) if i == j else block
    for i in range(blocks):
        inverse = inverse_factor([a[i, i][8 * t : 8 * t + 8, :] for t in range(q // 8)])
        for t in range(q // 8):
            linv[8 * t : 8 * t + 8, :] = inverse[t]
        li = split3(linv[...])

        def panel(first, last):
            block = jnp.concatenate([a[i, j][...] for j in range(first, last)], 1)
            return dot_six(li, split3(block), NN)

        pieces = []
        if i + 1 < blocks:
            pieces.append(panel(i + 1, i + 2))
            next_parts = split3(pieces[0])
            a[i + 1, i + 1][...] -= dot_six(next_parts, next_parts, TN)
        pieces.append(panel(i + len(pieces) + 1, blocks + 1))
        row = split3(jnp.concatenate(pieces, 1))
        cut = lambda first, last: [v[:, (first - i - 1) * q : (last - i - 1) * q] for v in row]
        for j in range(i + 1, blocks):
            first = j + 1 if j == i + 1 else j
            change = dot_six(cut(j, j + 1), cut(first, blocks + 1), TN)
            for c in range(first, blocks + 1):
                a[j, c][...] -= change[:, (c - first) * q : (c - first + 1) * q]
        z.append(dot_six(li, row, TN))
        z_parts = split3(z[i])
        for j in range(i):
            z[j] = z[j][:, q:] - dot_six(split3(z[j][:, :q]), z_parts, NN)


def fit_kernel(counts, codes, x_hbm, y_hbm, *refs, parts, blocks, tile):
    given, o_hbm, e_ref = refs[:parts], refs[parts], refs[parts + 1]
    x, y, o, wide, acc, packed, linv, sems = refs[parts + 2 : parts + 10]
    tiles_of_a = refs[parts + 10 :]
    m, q = y.shape
    tiles = m // tile

    def moves(k):
        now = pl.ds(pl.multiple_of(k * tile, tile), tile)
        return (
            pltpu.make_async_copy(x_hbm.at[now, :], x.at[now, :], sems.at[0, k]),
            pltpu.make_async_copy(y_hbm.at[now, :], y.at[now, :], sems.at[1, k]),
            pltpu.make_async_copy(o.at[now, :], o_hbm.at[now, :], sems.at[2, k]),
        )

    for k in range(tiles):
        for copy in moves(k)[:2]:
            copy.start()
    z = []
    solve_into(z, counts, codes, given, packed, linv, tiles_of_a)
    for i in range(blocks):
        here = slice(i * q, (i + 1) * q)
        wide[here, :q], wide[here, q:] = split(z[i])
    acc[...] = jnp.zeros_like(acc)
    valid = valid_rows(counts, m)

    @pl.loop(0, tiles)
    def _(k):
        x_in, y_in, out = moves(k)
        x_in.wait()
        y_in.wait()
        now = pl.ds(pl.multiple_of(k * tile, tile), tile)
        keep = lax.broadcasted_iota(jnp.int32, (tile, 1), 0) < valid - k * tile
        h, l = split(x[now, :])
        both = dot_bf(h, wide[...], NN)
        value = both[:, :q] + (both[:, q:] + dot_bf(l, wide[:, :q], NN))
        value = jnp.where(keep, value, 0.0)
        o[now, :] = value.astype(BF)
        out.start()
        gap = jnp.where(keep, y[now, :] - value, 0.0)
        acc[...] += jnp.sum((gap * gap).reshape(tile // 8, 8, q), axis=0)

    share = counts[lax.axis_index("tm")].astype(F32) * q
    e_ref[...] = jnp.broadcast_to(jnp.sum(acc[...]) / share, (1, q))

    @pl.loop(0, tiles)
    def _(k):
        moves(k)[2].wait()


def fit(counts, codes, x, y, given):
    m, f = x.shape
    q = y.shape[1]
    blocks, parts, tile = f // q, len(given), math.gcd(m, 1024)
    smem, vmem, hbm = (pl.BlockSpec(memory_space=s) for s in (pltpu.SMEM, pltpu.VMEM, pl.ANY))
    return pl.pallas_call(
        functools.partial(fit_kernel, blocks=blocks, parts=parts, tile=tile),
        out_shape=(pltpu.HBM((m, q), BF), jax.ShapeDtypeStruct((1, q), F32)),
        in_specs=[smem, smem, hbm, hbm] + [vmem] * parts,
        out_specs=(hbm, vmem),
        scratch_shapes=[
            pltpu.VMEM((m, f), F32),
            pltpu.VMEM((m, q), F32),
            pltpu.VMEM((m, q), BF),
            pltpu.VMEM((f, 2 * q), BF),
            pltpu.VMEM((8, q), F32),
            pltpu.VMEM((parts * given[0].shape[0], q), F32),
            pltpu.VMEM((q, q), F32),
            pltpu.SemaphoreType.DMA((3, m // tile)),
        ]
        + [pltpu.VMEM((q, q), F32)] * (blocks * (blocks + 1) // 2 + blocks),
        compiler_params=pltpu.CompilerParams(vmem_limit_bytes=FIT_VMEM),
        name="fit",
    )(counts, codes, in_hbm(x), in_hbm(y), *given)


def swap(value, axes, size, j):
    return lax.ppermute(value, axes, [(i, i ^ j) for i in range(size)])


def total(values):
    return functools.reduce(jnp.add, values)


def earlier_sums(mine, sent, n_time, n_rows):
    sub_parts = n_rows
    part_rows = mine.shape[0] // sub_parts
    core_swap = lambda v: swap(v, "rows", n_rows, 1)
    n_seats = n_rows // 2
    time_index = lax.axis_index("tm")
    odd = time_index % 2

    def seat_swap(value, j):
        late, seat = divmod(j, n_seats)
        pairs = [
            (t * n_rows + r, (t ^ late) * n_rows + (r ^ (2 * seat))) for t in range(n_time) for r in range(n_rows)
        ]
        return lax.ppermute(value, ("tm", "rows"), pairs)

    mine = mine + core_swap(sent)
    slots = [mine[j * part_rows : (j + 1) * part_rows] for j in range(sub_parts)]
    slots = [slots[0]] + [seat_swap(slots[j], j) for j in range(1, sub_parts)]
    same, other = total(slots[:n_seats]), total(slots[n_seats:])
    both = same + other
    even_part = jnp.where(odd == 1, other, same)
    group = time_index // 2
    before = jnp.zeros_like(both)
    for j in range(1, n_time // 2):
        came = swap(both, "tm", n_time, 2 * j)
        before = before + jnp.where((group ^ j) < group, came, 0.0)
    with_even = before + even_part
    for_same = jnp.where(odd == 1, with_even, before)
    for_other = jnp.where(odd == 1, before, with_even)
    out = [for_same] + [seat_swap(for_same if j < n_seats else for_other, j) for j in range(1, sub_parts)]
    return out + [core_swap(v) for v in out]


def body(features, response_lines, row_counts, ridge_codes, n_time, n_rows):
    mine, sent = gram(row_counts, features, response_lines, n_rows)
    given = earlier_sums(mine, sent, n_time, n_rows)
    forecast, error = fit(row_counts, ridge_codes, features, response_lines, given)
    partition_mse = total([error] + [swap(error, "rows", n_rows, j) for j in range(1, n_rows)])
    return forecast, partition_mse[0, :1]


def solution(mesh):
    return jax.shard_map(
        functools.partial(body, n_time=mesh.shape["tm"], n_rows=mesh.shape["rows"]),
        mesh=mesh,
        in_specs=(P(("tm", "rows"), None), P(("tm", "rows"), None), P(), P()),
        out_specs=(P(("tm", "rows"), None), P("tm")),
        check_vma=False,
    )
```

```python
import functools
import math

import jax
import jax.numpy as jnp
from jax import lax
from jax.experimental import pallas as pl
from jax.experimental.pallas import tpu as pltpu
from jax.sharding import PartitionSpec as P

GRAM_VMEM, FIT_VMEM = 48 << 20, 48 << 20
BF = jnp.bfloat16
F32 = jnp.float32
NN = (((1,), (0,)), ((), ()))
TN = (((0,), (0,)), ((), ()))


def in_hbm(value):
    return pltpu.with_memory_space_constraint(value, pltpu.HBM)


def split(value):
    high = value.astype(BF)
    return high, (value - high.astype(F32)).astype(BF)


def dot_bf(a, b, dims):
    return lax.dot_general(a, b, dims, preferred_element_type=F32)


def slot_of(piece, part_rows, sub_parts, place, row):
    part, offset = divmod(row, part_rows)
    half, sub = divmod(part, sub_parts)
    return half, pl.ds(pl.multiple_of((sub ^ place) * part_rows + offset, 8), piece)


def seat(n_rows):
    time_index, row_index = lax.axis_index("tm"), lax.axis_index("rows")
    return row_index % 2, (time_index % 2) * (n_rows // 2) + row_index // 2


def valid_rows(counts, m):
    left = counts[lax.axis_index("tm")] - lax.axis_index("rows") * m
    return jnp.minimum(jnp.maximum(left, 0), m)


def gram_kernel(counts, x_hbm, y_hbm, mine_ref, send_ref, x, y, wide, left, cross, sems, *, sub_parts):
    (m, f), q = x.shape, y.shape[1]
    half, blocks = f // 2, f // q
    chunks = sems.shape[1]
    chunk = m // chunks
    part_rows = mine_ref.shape[0] // sub_parts

    def moves(k):
        now = pl.ds(pl.multiple_of(k * chunk, chunk), chunk)
        return (
            pltpu.make_async_copy(x_hbm.at[now, :], x.at[now, :], sems.at[0, k]),
            pltpu.make_async_copy(y_hbm.at[now, :], y.at[now, :], sems.at[1, k]),
        )

    for k in range(chunks):
        for copy in moves(k):
            copy.start()
    for ref in (wide, left, cross):
        ref[...] = jnp.zeros_like(ref)
    valid = valid_rows(counts, m)

    def add(first, count):
        rows = count * chunk
        for k in range(count):
            for copy in moves(first + k):
                copy.wait()
        now = pl.ds(pl.multiple_of(first * chunk, chunk), rows)
        keep = lax.broadcasted_iota(jnp.int32, (rows, 1), 0) < valid - first * chunk
        h, l = split(jnp.where(keep, x[now, :], 0.0))
        yh, yl = split(jnp.where(keep, y[now, :], 0.0))
        wide[...] += dot_bf(h, jnp.concatenate([h[:, half:], l, yh, yl], 1), TN)
        left[...] += dot_bf(h[:, :half], h[:, :half], TN)
        cross[...] += dot_bf(yh, l, TN)

    count = math.gcd(chunks, 4)
    if count == 4:
        add(0, 1)
        add(1, 3)
    else:
        add(0, count)

    @pl.loop(1, chunks // count)
    def _(k):
        add(k * count, count)

    core, place = seat(sub_parts)
    piece = math.gcd(part_rows, q)

    def put(at, block):
        for r in range(0, q, piece):
            owner, where = slot_of(piece, part_rows, sub_parts, place, at + r)

            @pl.when(core == owner)
            def _(r=r, where=where):
                mine_ref[where, :] = block[r : r + piece]

            @pl.when(core != owner)
            def _(r=r, where=where):
                send_ref[where, :] = block[r : r + piece]

    at = 0
    for i in range(blocks):
        si = slice(i * q, (i + 1) * q)
        for j in range(i, blocks):
            sj = slice(j * q, (j + 1) * q)
            high = left[si, sj] if (j + 1) * q <= half else wide[si, j * q - half : (j + 1) * q - half]
            low = wide[si, half + j * q : half + (j + 1) * q]
            put(at, high + (low + wide[sj, half + i * q : half + (i + 1) * q].T))
            at += q
    for i in range(blocks):
        si = slice(i * q, (i + 1) * q)
        put(at, wide[si, half + f : half + f + q] + (wide[si, half + f + q :] + cross[:, si].T))
        at += q


def gram(counts, x, y, sub_parts):
    m, f = x.shape
    q = y.shape[1]
    blocks = f // q
    rows = (blocks * (blocks + 1) // 2 + blocks) * q
    smem, vmem, hbm = (pl.BlockSpec(memory_space=s) for s in (pltpu.SMEM, pltpu.VMEM, pl.ANY))
    return pl.pallas_call(
        functools.partial(gram_kernel, sub_parts=sub_parts),
        out_shape=[jax.ShapeDtypeStruct((rows // 2, q), F32)] * 2,
        in_specs=[smem, hbm, hbm],
        out_specs=[vmem, vmem],
        scratch_shapes=[
            pltpu.VMEM((m, f), F32),
            pltpu.VMEM((m, q), F32),
            pltpu.VMEM((f, f // 2 + f + 2 * q), F32),
            pltpu.VMEM((f // 2, f // 2), F32),
            pltpu.VMEM((q, f), F32),
            pltpu.SemaphoreType.DMA((2, m // math.gcd(m, 512))),
        ],
        compiler_params=pltpu.CompilerParams(vmem_limit_bytes=GRAM_VMEM),
        name="gram",
    )(in_hbm(counts), in_hbm(x), in_hbm(y))


def inverse_factor(groups, span=4):
    count, shape = len(groups), groups[0].shape
    lane = lax.broadcasted_iota(jnp.int32, shape, 1)
    sub = lax.broadcasted_iota(jnp.int32, shape, 0)
    spread = lambda v: jnp.broadcast_to(v, shape)
    out = []
    for k in range(0, count, span):
        c0, width = 8 * k, 8 * span
        inside = (lane >= c0) & (lane < c0 + width)
        col = [[spread(groups[k + g][:, c0 + c : c0 + c + 1]) for c in range(8 * g + 8)] for g in range(span)]
        col[0][0] = col[0][0] + 0.0
        rows = [
            jnp.where(inside, jnp.where(lane - c0 - 8 * g == sub, 1.0, 0.0), groups[k + g]) for g in range(span)
        ]
        for b in range(width):
            g0, r = divmod(b, 8)
            scale = lax.rsqrt(spread(col[g0][b][r : r + 1, :]))
            factor = {g: col[g][b] * scale for g in range(g0, span)}
            for c in range(b + 1, width):
                gc, rc = divmod(c, 8)
                other = spread(factor[gc][rc : rc + 1, :])
                for g in range(gc, span):
                    col[g][c] = col[g][c] - factor[g] * other
            u = spread(rows[g0][r : r + 1, :]) * scale
            rows[g0] = jnp.where(sub == r, u, rows[g0] - jnp.where(sub > r, factor[g0], 0.0) * u)
            for g in range(g0 + 1, span):
                rows[g] = rows[g] - factor[g] * u
        out += [jnp.where(lane < c0 + width, v, 0.0) for v in rows]
        if k + span < count:
            h, l = split(jnp.concatenate(rows, 0))
            change = dot_bf(jnp.concatenate([h, h, l], 0), jnp.concatenate([h, l, h], 0), TN)
            for g in range(k + span, count):
                groups[g] = jnp.where(inside, 0.0, groups[g]) - change[8 * g : 8 * g + 8]
    return out


def split3(value):
    high = value.astype(BF)
    rest = value - high.astype(F32)
    return (high,) + split(rest)


def dot_six(a, b, dims):
    left = jnp.concatenate([a[i] for i in (0, 0, 1, 0, 2, 1)], dims[0][0][0])
    right = jnp.concatenate([b[i] for i in (0, 1, 0, 2, 0, 1)], dims[0][1][0])
    return dot_bf(left, right, dims)


def solve_into(z, counts, codes, given, packed, linv, tiles):
    parts = len(given)
    sub_parts = parts // 2
    part_rows, q = given[0].shape
    blocks = next(n for n in range(1, len(tiles) + 1) if n * (n + 1) // 2 + n == len(tiles))
    previous = jnp.maximum(lax.axis_index("tm") - 1, 0)
    seen = lax.fori_loop(0, previous + 1, lambda k, t: t + counts[k], jnp.int32(0))
    ridge = codes[previous].astype(F32) * seen.astype(F32) / 16.0
    core, place = seat(sub_parts)
    for slot in range(parts):
        half, sub = divmod(slot, sub_parts)
        part = (half ^ core) * sub_parts + (sub ^ place)
        packed[pl.ds(pl.multiple_of(part * part_rows, 8), part_rows), :] = given[slot][...]
    eye = lax.broadcasted_iota(jnp.int32, (q, q), 0) == lax.broadcasted_iota(jnp.int32, (q, q), 1)
    order = [(i, j) for i in range(blocks) for j in range(i, blocks)] + [(i, blocks) for i in range(blocks)]
    a = {}
    for n, (i, j) in enumerate(order):
        block = packed[n * q : (n + 1) * q, :]
        a[i, j] = tiles[n]
        a[i, j][...] = block + jnp.where(eye, ridge, 0.0) if i == j else block
    for i in range(blocks):
        inverse = inverse_factor([a[i, i][8 * t : 8 * t + 8, :] for t in range(q // 8)])
        for t in range(q // 8):
            linv[8 * t : 8 * t + 8, :] = inverse[t]
        li = split3(linv[...])

        def panel(first, last):
            block = jnp.concatenate([a[i, j][...] for j in range(first, last)], 1)
            return dot_six(li, split3(block), NN)

        pieces = []
        if i + 1 < blocks:
            pieces.append(panel(i + 1, i + 2))
            next_parts = split3(pieces[0])
            a[i + 1, i + 1][...] -= dot_six(next_parts, next_parts, TN)
        pieces.append(panel(i + len(pieces) + 1, blocks + 1))
        row = split3(jnp.concatenate(pieces, 1))
        cut = lambda first, last: [v[:, (first - i - 1) * q : (last - i - 1) * q] for v in row]
        for j in range(i + 1, blocks):
            first = j + 1 if j == i + 1 else j
            change = dot_six(cut(j, j + 1), cut(first, blocks + 1), TN)
            for c in range(first, blocks + 1):
                a[j, c][...] -= change[:, (c - first) * q : (c - first + 1) * q]
        z.append(dot_six(li, row, TN))
        z_parts = split3(z[i])
        for j in range(i):
            z[j] = z[j][:, q:] - dot_six(split3(z[j][:, :q]), z_parts, NN)


def fit_kernel(counts, codes, x_hbm, y_hbm, *refs, parts, blocks, tile):
    given, o_hbm, e_ref = refs[:parts], refs[parts], refs[parts + 1]
    x, y, o, wide, acc, packed, linv, sems = refs[parts + 2 : parts + 10]
    tiles_of_a = refs[parts + 10 :]
    m, q = y.shape
    tiles = m // tile

    def moves(k):
        now = pl.ds(pl.multiple_of(k * tile, tile), tile)
        return (
            pltpu.make_async_copy(x_hbm.at[now, :], x.at[now, :], sems.at[0, k]),
            pltpu.make_async_copy(y_hbm.at[now, :], y.at[now, :], sems.at[1, k]),
            pltpu.make_async_copy(o.at[now, :], o_hbm.at[now, :], sems.at[2, k]),
        )

    for k in range(tiles):
        for copy in moves(k)[:2]:
            copy.start()
    z = []
    solve_into(z, counts, codes, given, packed, linv, tiles_of_a)
    for i in range(blocks):
        here = slice(i * q, (i + 1) * q)
        wide[here, :q], wide[here, q:] = split(z[i])
    acc[...] = jnp.zeros_like(acc)
    valid = valid_rows(counts, m)

    @pl.loop(0, tiles)
    def _(k):
        x_in, y_in, out = moves(k)
        x_in.wait()
        y_in.wait()
        now = pl.ds(pl.multiple_of(k * tile, tile), tile)
        keep = lax.broadcasted_iota(jnp.int32, (tile, 1), 0) < valid - k * tile
        h, l = split(x[now, :])
        both = dot_bf(h, wide[...], NN)
        value = both[:, :q] + (both[:, q:] + dot_bf(l, wide[:, :q], NN))
        value = jnp.where(keep, value, 0.0)
        o[now, :] = value.astype(BF)
        out.start()
        gap = jnp.where(keep, y[now, :] - value, 0.0)
        acc[...] += jnp.sum((gap * gap).reshape(tile // 8, 8, q), axis=0)

    share = counts[lax.axis_index("tm")].astype(F32) * q
    e_ref[...] = jnp.broadcast_to(jnp.sum(acc[...]) / share, (1, q))

    @pl.loop(0, tiles)
    def _(k):
        moves(k)[2].wait()


def fit(counts, codes, x, y, given):
    m, f = x.shape
    q = y.shape[1]
    blocks, parts, tile = f // q, len(given), math.gcd(m, 2048)
    smem, vmem, hbm = (pl.BlockSpec(memory_space=s) for s in (pltpu.SMEM, pltpu.VMEM, pl.ANY))
    return pl.pallas_call(
        functools.partial(fit_kernel, blocks=blocks, parts=parts, tile=tile),
        out_shape=(pltpu.HBM((m, q), BF), jax.ShapeDtypeStruct((1, q), F32)),
        in_specs=[smem, smem, hbm, hbm] + [vmem] * parts,
        out_specs=(hbm, vmem),
        scratch_shapes=[
            pltpu.VMEM((m, f), F32),
            pltpu.VMEM((m, q), F32),
            pltpu.VMEM((m, q), BF),
            pltpu.VMEM((f, 2 * q), BF),
            pltpu.VMEM((8, q), F32),
            pltpu.VMEM((parts * given[0].shape[0], q), F32),
            pltpu.VMEM((q, q), F32),
            pltpu.SemaphoreType.DMA((3, m // tile)),
        ]
        + [pltpu.VMEM((q, q), F32)] * (blocks * (blocks + 1) // 2 + blocks),
        compiler_params=pltpu.CompilerParams(vmem_limit_bytes=FIT_VMEM),
        name="fit",
    )(counts, codes, in_hbm(x), in_hbm(y), *given)


def swap(value, axes, size, j):
    return lax.ppermute(value, axes, [(i, i ^ j) for i in range(size)])


def total(values):
    return functools.reduce(jnp.add, values)


def earlier_sums(mine, sent, n_time, n_rows):
    sub_parts = n_rows
    part_rows = mine.shape[0] // sub_parts
    core_swap = lambda v: swap(v, "rows", n_rows, 1)
    n_seats = n_rows // 2
    time_index = lax.axis_index("tm")
    odd = time_index % 2

    def seat_swap(value, j):
        late, seat = divmod(j, n_seats)
        pairs = [
            (t * n_rows + r, (t ^ late) * n_rows + (r ^ (2 * seat))) for t in range(n_time) for r in range(n_rows)
        ]
        return lax.ppermute(value, ("tm", "rows"), pairs)

    mine = mine + core_swap(sent)
    slots = [mine[j * part_rows : (j + 1) * part_rows] for j in range(sub_parts)]
    slots = [slots[0]] + [seat_swap(slots[j], j) for j in range(1, sub_parts)]
    same, other = total(slots[:n_seats]), total(slots[n_seats:])
    both = same + other
    even_part = jnp.where(odd == 1, other, same)
    group = time_index // 2
    before = jnp.zeros_like(both)
    for j in range(1, n_time // 2):
        came = swap(both, "tm", n_time, 2 * j)
        before = before + jnp.where((group ^ j) < group, came, 0.0)
    with_even = before + even_part
    for_same = jnp.where(odd == 1, with_even, before)
    for_other = jnp.where(odd == 1, before, with_even)
    out = [for_same] + [seat_swap(for_same if j < n_seats else for_other, j) for j in range(1, sub_parts)]
    return out + [core_swap(v) for v in out]


def body(features, response_lines, row_counts, ridge_codes, n_time, n_rows):
    mine, sent = gram(row_counts, features, response_lines, n_rows)
    given = earlier_sums(mine, sent, n_time, n_rows)
    forecast, error = fit(row_counts, ridge_codes, features, response_lines, given)
    partition_mse = total([error] + [swap(error, "rows", n_rows, j) for j in range(1, n_rows)])
    return forecast, partition_mse[0, :1]


def solution(mesh):
    return jax.shard_map(
        functools.partial(body, n_time=mesh.shape["tm"], n_rows=mesh.shape["rows"]),
        mesh=mesh,
        in_specs=(P(("tm", "rows"), None), P(("tm", "rows"), None), P(), P()),
        out_specs=(P(("tm", "rows"), None), P("tm")),
        check_vma=False,
    )
```

```python
import functools
import math

import jax
import jax.numpy as jnp
from jax import lax
from jax.experimental import pallas as pl
from jax.experimental.pallas import tpu as pltpu
from jax.sharding import PartitionSpec as P

GRAM_VMEM, FIT_VMEM = 48 << 20, 48 << 20
BF = jnp.bfloat16
F32 = jnp.float32
NN = (((1,), (0,)), ((), ()))
TN = (((0,), (0,)), ((), ()))


def in_hbm(value):
    return pltpu.with_memory_space_constraint(value, pltpu.HBM)


def split(value):
    high = value.astype(BF)
    return high, (value - high.astype(F32)).astype(BF)


def dot_bf(a, b, dims):
    return lax.dot_general(a, b, dims, preferred_element_type=F32)


def slot_of(piece, part_rows, sub_parts, place, row):
    part, offset = divmod(row, part_rows)
    half, sub = divmod(part, sub_parts)
    return half, pl.ds(pl.multiple_of((sub ^ place) * part_rows + offset, 8), piece)


def seat(n_rows):
    time_index, row_index = lax.axis_index("tm"), lax.axis_index("rows")
    return row_index % 2, (time_index % 2) * (n_rows // 2) + row_index // 2


def valid_rows(counts, m):
    left = counts[lax.axis_index("tm")] - lax.axis_index("rows") * m
    return jnp.minimum(jnp.maximum(left, 0), m)


def gram_kernel(counts, x_hbm, y_hbm, mine_ref, send_ref, x, y, wide, left, cross, sems, *, sub_parts):
    (m, f), q = x.shape, y.shape[1]
    half, blocks = f // 2, f // q
    chunks = sems.shape[1]
    chunk = m // chunks
    part_rows = mine_ref.shape[0] // sub_parts

    def moves(k):
        now = pl.ds(pl.multiple_of(k * chunk, chunk), chunk)
        return (
            pltpu.make_async_copy(x_hbm.at[now, :], x.at[now, :], sems.at[0, k]),
            pltpu.make_async_copy(y_hbm.at[now, :], y.at[now, :], sems.at[1, k]),
        )

    for k in range(chunks):
        for copy in moves(k):
            copy.start()
    for ref in (wide, left, cross):
        ref[...] = jnp.zeros_like(ref)
    valid = valid_rows(counts, m)

    def add(first, count):
        rows = count * chunk
        for k in range(count):
            for copy in moves(first + k):
                copy.wait()
        now = pl.ds(pl.multiple_of(first * chunk, chunk), rows)
        keep = lax.broadcasted_iota(jnp.int32, (rows, 1), 0) < valid - first * chunk
        h, l = split(jnp.where(keep, x[now, :], 0.0))
        yh, yl = split(jnp.where(keep, y[now, :], 0.0))
        wide[...] += dot_bf(h, jnp.concatenate([h[:, half:], l, yh, yl], 1), TN)
        left[...] += dot_bf(h[:, :half], h[:, :half], TN)
        cross[...] += dot_bf(yh, l, TN)

    count = math.gcd(chunks, 4)
    if count == 4:
        add(0, 1)
        add(1, 3)
    else:
        add(0, count)

    @pl.loop(1, chunks // count)
    def _(k):
        add(k * count, count)

    core, place = seat(sub_parts)
    piece = math.gcd(part_rows, q)

    def pack(kept_half):
        def put(at, block):
            for r in range(0, q, piece):
                owner, where = slot_of(piece, part_rows, sub_parts, place, at + r)
                target = mine_ref if owner == kept_half else send_ref
                target[where, :] = block[r : r + piece]

        at = 0
        for i in range(blocks):
            si = slice(i * q, (i + 1) * q)
            for j in range(i, blocks):
                sj = slice(j * q, (j + 1) * q)
                high = left[si, sj] if (j + 1) * q <= half else wide[si, j * q - half : (j + 1) * q - half]
                low = wide[si, half + j * q : half + (j + 1) * q]
                put(at, high + (low + wide[sj, half + i * q : half + (i + 1) * q].T))
                at += q
        for i in range(blocks):
            si = slice(i * q, (i + 1) * q)
            put(at, wide[si, half + f : half + f + q] + (wide[si, half + f + q :] + cross[:, si].T))
            at += q

    for c in range(2):
        pl.when(core == c)(functools.partial(pack, c))


def gram(counts, x, y, sub_parts):
    m, f = x.shape
    q = y.shape[1]
    blocks = f // q
    rows = (blocks * (blocks + 1) // 2 + blocks) * q
    smem, vmem, hbm = (pl.BlockSpec(memory_space=s) for s in (pltpu.SMEM, pltpu.VMEM, pl.ANY))
    return pl.pallas_call(
        functools.partial(gram_kernel, sub_parts=sub_parts),
        out_shape=[jax.ShapeDtypeStruct((rows // 2, q), F32)] * 2,
        in_specs=[smem, hbm, hbm],
        out_specs=[vmem, vmem],
        scratch_shapes=[
            pltpu.VMEM((m, f), F32),
            pltpu.VMEM((m, q), F32),
            pltpu.VMEM((f, f // 2 + f + 2 * q), F32),
            pltpu.VMEM((f // 2, f // 2), F32),
            pltpu.VMEM((q, f), F32),
            pltpu.SemaphoreType.DMA((2, m // math.gcd(m, 512))),
        ],
        compiler_params=pltpu.CompilerParams(vmem_limit_bytes=GRAM_VMEM),
        name="gram",
    )(in_hbm(counts), in_hbm(x), in_hbm(y))


def inverse_factor(groups, kept, span=4):
    count, shape = len(groups), groups[0].shape
    lane = lax.broadcasted_iota(jnp.int32, shape, 1)
    sub = lax.broadcasted_iota(jnp.int32, shape, 0)
    spread = lambda v: jnp.broadcast_to(v, shape)
    out = []
    for k in range(0, count, span):
        c0, width = 8 * k, 8 * span
        inside = (lane >= c0) & (lane < c0 + width)
        col = [[spread(groups[k + g][:, c0 + c : c0 + c + 1]) for c in range(8 * g + 8)] for g in range(span)]
        col[0][0] = col[0][0] + 0.0
        entry = lambda a, b: spread(col[a // 8][b][a % 8 : a % 8 + 1, :])
        pivot = entry(0, 0)
        rows = [
            jnp.where(inside, jnp.where(lane - c0 - 8 * g == sub, 1.0, 0.0), groups[k + g]) for g in range(span)
        ]
        for b in range(width):
            g0, r = divmod(b, 8)
            scale = lax.rsqrt(pivot)
            factor = {g: col[g][b] * scale for g in range(g0, span)}
            for g in range(g0, span):
                kept[b, 8 * g : 8 * g + 8, :] = factor[g]
            if b + 1 < width:
                first = entry(b + 1, b) * scale
                pivot = entry(b + 1, b + 1) - first * first
            for c in range(b + 1, width):
                other = first if c == b + 1 else kept[b, pl.ds(c, 8, stride=0), :]
                for g in range(c // 8, span):
                    col[g][c] = col[g][c] - factor[g] * other
            u = spread(rows[g0][r : r + 1, :]) * scale
            rows[g0] = jnp.where(sub == r, u, rows[g0] - jnp.where(sub > r, factor[g0], 0.0) * u)
            for g in range(g0 + 1, span):
                rows[g] = rows[g] - factor[g] * u
        out += [jnp.where(lane < c0 + width, v, 0.0) for v in rows]
        if k + span < count:
            h, l = split(jnp.concatenate(rows, 0))
            change = dot_bf(jnp.concatenate([h, h, l], 0), jnp.concatenate([h, l, h], 0), TN)
            for g in range(k + span, count):
                groups[g] = jnp.where(inside, 0.0, groups[g]) - change[8 * g : 8 * g + 8]
    return out


def split3(value):
    high = value.astype(BF)
    rest = value - high.astype(F32)
    return (high,) + split(rest)


def dot_six(a, b, dims):
    left = jnp.concatenate([a[i] for i in (0, 0, 1, 0, 2, 1)], dims[0][0][0])
    right = jnp.concatenate([b[i] for i in (0, 1, 0, 2, 0, 1)], dims[0][1][0])
    return dot_bf(left, right, dims)


def solve_into(z, counts, codes, given, packed, linv, kept, tiles):
    parts = len(given)
    sub_parts = parts // 2
    part_rows, q = given[0].shape
    blocks = next(n for n in range(1, len(tiles) + 1) if n * (n + 1) // 2 + n == len(tiles))
    previous = jnp.maximum(lax.axis_index("tm") - 1, 0)
    seen = lax.fori_loop(0, previous + 1, lambda k, t: t + counts[k], jnp.int32(0))
    ridge = codes[previous].astype(F32) * seen.astype(F32) / 16.0
    core, place = seat(sub_parts)
    for slot in range(parts):
        half, sub = divmod(slot, sub_parts)
        part = (half ^ core) * sub_parts + (sub ^ place)
        packed[pl.ds(pl.multiple_of(part * part_rows, 8), part_rows), :] = given[slot][...]
    eye = lax.broadcasted_iota(jnp.int32, (q, q), 0) == lax.broadcasted_iota(jnp.int32, (q, q), 1)
    order = [(i, j) for i in range(blocks) for j in range(i, blocks)] + [(i, blocks) for i in range(blocks)]
    a = {}
    for n, (i, j) in enumerate(order):
        block = packed[n * q : (n + 1) * q, :]
        a[i, j] = tiles[n]
        a[i, j][...] = block + jnp.where(eye, ridge, 0.0) if i == j else block
    for i in range(blocks):
        inverse = inverse_factor([a[i, i][8 * t : 8 * t + 8, :] for t in range(q // 8)], kept)
        for t in range(q // 8):
            linv[8 * t : 8 * t + 8, :] = inverse[t]
        li = split3(linv[...])

        def panel(first, last):
            block = jnp.concatenate([a[i, j][...] for j in range(first, last)], 1)
            return dot_six(li, split3(block), NN)

        pieces = []
        if i + 1 < blocks:
            pieces.append(panel(i + 1, i + 2))
            next_parts = split3(pieces[0])
            a[i + 1, i + 1][...] -= dot_six(next_parts, next_parts, TN)
        pieces.append(panel(i + len(pieces) + 1, blocks + 1))
        row = split3(jnp.concatenate(pieces, 1))
        cut = lambda first, last: [v[:, (first - i - 1) * q : (last - i - 1) * q] for v in row]
        for j in range(i + 1, blocks):
            first = j + 1 if j == i + 1 else j
            change = dot_six(cut(j, j + 1), cut(first, blocks + 1), TN)
            for c in range(first, blocks + 1):
                a[j, c][...] -= change[:, (c - first) * q : (c - first + 1) * q]
        z.append(dot_six(li, row, TN))
        z_parts = split3(z[i])
        for j in range(i):
            z[j] = z[j][:, q:] - dot_six(split3(z[j][:, :q]), z_parts, NN)


def fit_kernel(counts, codes, x_hbm, y_hbm, *refs, parts, blocks, tile):
    given, o_hbm, e_ref = refs[:parts], refs[parts], refs[parts + 1]
    x, y, o, wide, acc, packed, linv, kept, sems = refs[parts + 2 : parts + 11]
    tiles_of_a = refs[parts + 11 :]
    m, q = y.shape
    tiles = m // tile

    def moves(k):
        now = pl.ds(pl.multiple_of(k * tile, tile), tile)
        return (
            pltpu.make_async_copy(x_hbm.at[now, :], x.at[now, :], sems.at[0, k]),
            pltpu.make_async_copy(y_hbm.at[now, :], y.at[now, :], sems.at[1, k]),
            pltpu.make_async_copy(o.at[now, :], o_hbm.at[now, :], sems.at[2, k]),
        )

    for k in range(tiles):
        for copy in moves(k)[:2]:
            copy.start()
    z = []
    solve_into(z, counts, codes, given, packed, linv, kept, tiles_of_a)
    for i in range(blocks):
        here = slice(i * q, (i + 1) * q)
        wide[here, :q], wide[here, q:] = split(z[i])
    acc[...] = jnp.zeros_like(acc)
    valid = valid_rows(counts, m)

    @pl.loop(0, tiles)
    def _(k):
        x_in, y_in, out = moves(k)
        x_in.wait()
        y_in.wait()
        now = pl.ds(pl.multiple_of(k * tile, tile), tile)
        left = valid - k * tile

        def predict(limit):
            h, l = split(x[now, :])
            both = dot_bf(h, wide[...], NN)
            value = limit(both[:, :q] + (both[:, q:] + dot_bf(l, wide[:, :q], NN)))
            o[now, :] = value.astype(BF)
            gap = limit(y[now, :] - value)
            acc[...] += jnp.sum((gap * gap).reshape(tile // 8, 8, q), axis=0)

        @pl.when(left >= tile)
        def _():
            predict(lambda v: v)

        @pl.when((left > 0) & (left < tile))
        def _():
            keep = lax.broadcasted_iota(jnp.int32, (tile, q), 0) < left
            predict(lambda v: jnp.where(keep, v, 0.0))

        @pl.when(left <= 0)
        def _():
            o[now, :] = jnp.zeros((tile, q), BF)

        out.start()

    share = counts[lax.axis_index("tm")].astype(F32) * q
    e_ref[...] = jnp.broadcast_to(jnp.sum(acc[...]) / share, (1, q))

    @pl.loop(0, tiles)
    def _(k):
        moves(k)[2].wait()


def fit(counts, codes, x, y, given):
    m, f = x.shape
    q = y.shape[1]
    blocks, parts, tile = f // q, len(given), math.gcd(m, 2048)
    smem, vmem, hbm = (pl.BlockSpec(memory_space=s) for s in (pltpu.SMEM, pltpu.VMEM, pl.ANY))
    return pl.pallas_call(
        functools.partial(fit_kernel, blocks=blocks, parts=parts, tile=tile),
        out_shape=(pltpu.HBM((m, q), BF), jax.ShapeDtypeStruct((1, q), F32)),
        in_specs=[smem, smem, hbm, hbm] + [vmem] * parts,
        out_specs=(hbm, vmem),
        scratch_shapes=[
            pltpu.VMEM((m, f), F32),
            pltpu.VMEM((m, q), F32),
            pltpu.VMEM((m, q), BF),
            pltpu.VMEM((f, 2 * q), BF),
            pltpu.VMEM((8, q), F32),
            pltpu.VMEM((parts * given[0].shape[0], q), F32),
            pltpu.VMEM((q, q), F32),
            pltpu.VMEM((32, 32, q), F32),
            pltpu.SemaphoreType.DMA((3, m // tile)),
        ]
        + [pltpu.VMEM((q, q), F32)] * (blocks * (blocks + 1) // 2 + blocks),
        compiler_params=pltpu.CompilerParams(vmem_limit_bytes=FIT_VMEM),
        name="fit",
    )(counts, codes, in_hbm(x), in_hbm(y), *given)


def swap(value, axes, size, j):
    return lax.ppermute(value, axes, [(i, i ^ j) for i in range(size)])


def total(values):
    return functools.reduce(jnp.add, values)


def earlier_sums(mine, sent, n_time, n_rows):
    sub_parts = n_rows
    part_rows = mine.shape[0] // sub_parts
    core_swap = lambda v: swap(v, "rows", n_rows, 1)
    n_seats = n_rows // 2
    time_index = lax.axis_index("tm")
    odd = time_index % 2

    def seat_swap(value, j):
        late, seat = divmod(j, n_seats)
        pairs = [
            (t * n_rows + r, (t ^ late) * n_rows + (r ^ (2 * seat))) for t in range(n_time) for r in range(n_rows)
        ]
        return lax.ppermute(value, ("tm", "rows"), pairs)

    mine = mine + core_swap(sent)
    slots = [mine[j * part_rows : (j + 1) * part_rows] for j in range(sub_parts)]
    slots = [slots[0]] + [seat_swap(slots[j], j) for j in range(1, sub_parts)]
    same, other = total(slots[:n_seats]), total(slots[n_seats:])
    both = same + other
    even_part = jnp.where(odd == 1, other, same)
    group = time_index // 2
    before = jnp.zeros_like(both)
    for j in range(1, n_time // 2):
        came = swap(both, "tm", n_time, 2 * j)
        before = before + jnp.where((group ^ j) < group, came, 0.0)
    with_even = before + even_part
    for_same = jnp.where(odd == 1, with_even, before)
    for_other = jnp.where(odd == 1, before, with_even)
    out = [for_same] + [seat_swap(for_same if j < n_seats else for_other, j) for j in range(1, sub_parts)]
    return out + [core_swap(v) for v in out]


def body(features, response_lines, row_counts, ridge_codes, n_time, n_rows):
    mine, sent = gram(row_counts, features, response_lines, n_rows)
    given = earlier_sums(mine, sent, n_time, n_rows)
    forecast, error = fit(row_counts, ridge_codes, features, response_lines, given)
    partition_mse = total([error] + [swap(error, "rows", n_rows, j) for j in range(1, n_rows)])
    return forecast, partition_mse[0, :1]


def solution(mesh):
    return jax.shard_map(
        functools.partial(body, n_time=mesh.shape["tm"], n_rows=mesh.shape["rows"]),
        mesh=mesh,
        in_specs=(P(("tm", "rows"), None), P(("tm", "rows"), None), P(), P()),
        out_specs=(P(("tm", "rows"), None), P("tm")),
        check_vma=False,
    )
```

```python
import functools
import math

import jax
import jax.numpy as jnp
from jax import lax
from jax.experimental import pallas as pl
from jax.experimental.pallas import tpu as pltpu
from jax.sharding import PartitionSpec as P

GRAM_VMEM, FIT_VMEM = 48 << 20, 48 << 20
BF = jnp.bfloat16
F32 = jnp.float32
NN = (((1,), (0,)), ((), ()))
TN = (((0,), (0,)), ((), ()))


def in_hbm(value):
    return pltpu.with_memory_space_constraint(value, pltpu.HBM)


def split(value):
    high = value.astype(BF)
    return high, (value - high.astype(F32)).astype(BF)


def dot_bf(a, b, dims):
    return lax.dot_general(a, b, dims, preferred_element_type=F32)


def slot_of(piece, part_rows, sub_parts, place, row):
    part, offset = divmod(row, part_rows)
    half, sub = divmod(part, sub_parts)
    return half, pl.ds(pl.multiple_of((sub ^ place) * part_rows + offset, 8), piece)


def seat(n_rows):
    time_index, row_index = lax.axis_index("tm"), lax.axis_index("rows")
    return row_index % 2, (time_index % 2) * (n_rows // 2) + row_index // 2


def valid_rows(counts, m):
    left = counts[lax.axis_index("tm")] - lax.axis_index("rows") * m
    return jnp.minimum(jnp.maximum(left, 0), m)


def gram_kernel(counts, x_hbm, y_hbm, mine_ref, send_ref, x, y, wide, left, cross, sems, *, sub_parts):
    (m, f), q = x.shape, y.shape[1]
    half, blocks = f // 2, f // q
    chunks = sems.shape[1]
    chunk = m // chunks
    part_rows = mine_ref.shape[0] // sub_parts

    def moves(k):
        now = pl.ds(pl.multiple_of(k * chunk, chunk), chunk)
        return (
            pltpu.make_async_copy(x_hbm.at[now, :], x.at[now, :], sems.at[0, k]),
            pltpu.make_async_copy(y_hbm.at[now, :], y.at[now, :], sems.at[1, k]),
        )

    for k in range(chunks):
        for copy in moves(k):
            copy.start()
    for ref in (wide, left, cross):
        ref[...] = jnp.zeros_like(ref)
    valid = valid_rows(counts, m)

    def add(first, count):
        rows = count * chunk
        for k in range(count):
            for copy in moves(first + k):
                copy.wait()
        now = pl.ds(pl.multiple_of(first * chunk, chunk), rows)
        here = valid - first * chunk

        @pl.when((here > 0) & (here < rows))
        def _():
            for array in (x, y):
                keep = lax.broadcasted_iota(jnp.int32, (rows, array.shape[1]), 0) < here
                array[now, :] = jnp.where(keep, array[now, :], 0.0)

        @pl.when(here > 0)
        def _():
            h, l = split(x[now, :])
            yh, yl = split(y[now, :])
            wide[...] += dot_bf(h, jnp.concatenate([h[:, half:], l, yh, yl], 1), TN)
            left[...] += dot_bf(h[:, :half], h[:, :half], TN)
            cross[...] += dot_bf(yh, l, TN)

    count = math.gcd(chunks, 4)
    if count == 4:
        add(0, 1)
        add(1, 3)
    else:
        add(0, count)

    @pl.loop(1, chunks // count)
    def _(k):
        add(k * count, count)

    core, place = seat(sub_parts)
    piece = math.gcd(part_rows, q)

    def pack(kept_half):
        def put(at, block):
            for r in range(0, q, piece):
                owner, where = slot_of(piece, part_rows, sub_parts, place, at + r)
                target = mine_ref if owner == kept_half else send_ref
                target[where, :] = block[r : r + piece]

        at = 0
        for i in range(blocks):
            si = slice(i * q, (i + 1) * q)
            for j in range(i, blocks):
                sj = slice(j * q, (j + 1) * q)
                high = left[si, sj] if (j + 1) * q <= half else wide[si, j * q - half : (j + 1) * q - half]
                low = wide[si, half + j * q : half + (j + 1) * q]
                put(at, high + (low + wide[sj, half + i * q : half + (i + 1) * q].T))
                at += q
        for i in range(blocks):
            si = slice(i * q, (i + 1) * q)
            put(at, wide[si, half + f : half + f + q] + (wide[si, half + f + q :] + cross[:, si].T))
            at += q

    for c in range(2):
        pl.when(core == c)(functools.partial(pack, c))


def gram(counts, x, y, sub_parts):
    m, f = x.shape
    q = y.shape[1]
    blocks = f // q
    rows = (blocks * (blocks + 1) // 2 + blocks) * q
    smem, vmem, hbm = (pl.BlockSpec(memory_space=s) for s in (pltpu.SMEM, pltpu.VMEM, pl.ANY))
    return pl.pallas_call(
        functools.partial(gram_kernel, sub_parts=sub_parts),
        out_shape=[jax.ShapeDtypeStruct((rows // 2, q), F32)] * 2,
        in_specs=[smem, hbm, hbm],
        out_specs=[vmem, vmem],
        scratch_shapes=[
            pltpu.VMEM((m, f), F32),
            pltpu.VMEM((m, q), F32),
            pltpu.VMEM((f, f // 2 + f + 2 * q), F32),
            pltpu.VMEM((f // 2, f // 2), F32),
            pltpu.VMEM((q, f), F32),
            pltpu.SemaphoreType.DMA((2, m // math.gcd(m, 512))),
        ],
        compiler_params=pltpu.CompilerParams(vmem_limit_bytes=GRAM_VMEM),
        name="gram",
    )(in_hbm(counts), in_hbm(x), in_hbm(y))


def inverse_factor(groups, kept, span=4):
    count, shape = len(groups), groups[0].shape
    lane = lax.broadcasted_iota(jnp.int32, shape, 1)
    sub = lax.broadcasted_iota(jnp.int32, shape, 0)
    spread = lambda v: jnp.broadcast_to(v, shape)
    out = []
    for k in range(0, count, span):
        c0, width = 8 * k, 8 * span
        inside = (lane >= c0) & (lane < c0 + width)
        col = [[spread(groups[k + g][:, c0 + c : c0 + c + 1]) for c in range(8 * g + 8)] for g in range(span)]
        col[0][0] = col[0][0] + 0.0
        entry = lambda a, b: spread(col[a // 8][b][a % 8 : a % 8 + 1, :])
        pivot = entry(0, 0)
        rows = [
            jnp.where(inside, jnp.where(lane - c0 - 8 * g == sub, 1.0, 0.0), groups[k + g]) for g in range(span)
        ]
        for b in range(width):
            g0, r = divmod(b, 8)
            scale = lax.rsqrt(pivot)
            factor = {g: col[g][b] * scale for g in range(g0, span)}
            for g in range(g0, span):
                kept[b, 8 * g : 8 * g + 8, :] = factor[g]
            if b + 1 < width:
                first = entry(b + 1, b) * scale
                pivot = entry(b + 1, b + 1) - first * first
            for c in range(b + 1, width):
                other = first if c == b + 1 else kept[b, pl.ds(c, 8, stride=0), :]
                for g in range(c // 8, span):
                    col[g][c] = col[g][c] - factor[g] * other
            u = spread(rows[g0][r : r + 1, :]) * scale
            rows[g0] = jnp.where(sub == r, u, rows[g0] - jnp.where(sub > r, factor[g0], 0.0) * u)
            for g in range(g0 + 1, span):
                rows[g] = rows[g] - factor[g] * u
        out += [jnp.where(lane < c0 + width, v, 0.0) for v in rows]
        if k + span < count:
            h, l = split(jnp.concatenate(rows, 0))
            change = dot_bf(jnp.concatenate([h, h, l], 0), jnp.concatenate([h, l, h], 0), TN)
            for g in range(k + span, count):
                groups[g] = jnp.where(inside, 0.0, groups[g]) - change[8 * g : 8 * g + 8]
    return out


def split3(value):
    high = value.astype(BF)
    rest = value - high.astype(F32)
    return (high,) + split(rest)


def dot_six(a, b, dims):
    left = jnp.concatenate([a[i] for i in (0, 0, 1, 0, 2, 1)], dims[0][0][0])
    right = jnp.concatenate([b[i] for i in (0, 1, 0, 2, 0, 1)], dims[0][1][0])
    return dot_bf(left, right, dims)


def solve_into(z, counts, codes, given, packed, linv, kept, tiles):
    parts = len(given)
    sub_parts = parts // 2
    part_rows, q = given[0].shape
    blocks = next(n for n in range(1, len(tiles) + 1) if n * (n + 1) // 2 + n == len(tiles))
    previous = jnp.maximum(lax.axis_index("tm") - 1, 0)
    seen = lax.fori_loop(0, previous + 1, lambda k, t: t + counts[k], jnp.int32(0))
    ridge = codes[previous].astype(F32) * seen.astype(F32) / 16.0
    core, place = seat(sub_parts)
    for slot in range(parts):
        half, sub = divmod(slot, sub_parts)
        part = (half ^ core) * sub_parts + (sub ^ place)
        packed[pl.ds(pl.multiple_of(part * part_rows, 8), part_rows), :] = given[slot][...]
    eye = lax.broadcasted_iota(jnp.int32, (q, q), 0) == lax.broadcasted_iota(jnp.int32, (q, q), 1)
    order = [(i, j) for i in range(blocks) for j in range(i, blocks)] + [(i, blocks) for i in range(blocks)]
    a = {}
    for n, (i, j) in enumerate(order):
        block = packed[n * q : (n + 1) * q, :]
        a[i, j] = tiles[n]
        a[i, j][...] = block + jnp.where(eye, ridge, 0.0) if i == j else block
    for i in range(blocks):
        inverse = inverse_factor([a[i, i][8 * t : 8 * t + 8, :] for t in range(q // 8)], kept)
        for t in range(q // 8):
            linv[8 * t : 8 * t + 8, :] = inverse[t]
        li = split3(linv[...])

        def panel(first, last):
            block = jnp.concatenate([a[i, j][...] for j in range(first, last)], 1)
            return dot_six(li, split3(block), NN)

        pieces = []
        if i + 1 < blocks:
            pieces.append(panel(i + 1, i + 2))
            next_parts = split3(pieces[0])
            a[i + 1, i + 1][...] -= dot_six(next_parts, next_parts, TN)
        pieces.append(panel(i + len(pieces) + 1, blocks + 1))
        row = split3(jnp.concatenate(pieces, 1))
        cut = lambda first, last: [v[:, (first - i - 1) * q : (last - i - 1) * q] for v in row]
        for j in range(i + 1, blocks):
            first = j + 1 if j == i + 1 else j
            change = dot_six(cut(j, j + 1), cut(first, blocks + 1), TN)
            for c in range(first, blocks + 1):
                a[j, c][...] -= change[:, (c - first) * q : (c - first + 1) * q]
        z.append(dot_six(li, row, TN))
        z_parts = split3(z[i])
        for j in range(i):
            z[j] = z[j][:, q:] - dot_six(split3(z[j][:, :q]), z_parts, NN)


def fit_kernel(counts, codes, x_hbm, y_hbm, *refs, parts, blocks, tile):
    given, o_hbm, e_ref = refs[:parts], refs[parts], refs[parts + 1]
    x, y, o, wide, acc, packed, linv, kept, sems = refs[parts + 2 : parts + 11]
    tiles_of_a = refs[parts + 11 :]
    m, q = y.shape
    tiles = m // tile

    def moves(k):
        now = pl.ds(pl.multiple_of(k * tile, tile), tile)
        return (
            pltpu.make_async_copy(x_hbm.at[now, :], x.at[now, :], sems.at[0, k]),
            pltpu.make_async_copy(y_hbm.at[now, :], y.at[now, :], sems.at[1, k]),
            pltpu.make_async_copy(o.at[now, :], o_hbm.at[now, :], sems.at[2, k]),
        )

    for k in range(tiles):
        for copy in moves(k)[:2]:
            copy.start()
    z = []
    solve_into(z, counts, codes, given, packed, linv, kept, tiles_of_a)
    for i in range(blocks):
        here = slice(i * q, (i + 1) * q)
        wide[here, :q], wide[here, q:] = split(z[i])
    acc[...] = jnp.zeros_like(acc)
    valid = valid_rows(counts, m)

    @pl.loop(0, tiles)
    def _(k):
        x_in, y_in, out = moves(k)
        x_in.wait()
        y_in.wait()
        now = pl.ds(pl.multiple_of(k * tile, tile), tile)
        left = valid - k * tile

        def predict(limit):
            h, l = split(x[now, :])
            both = dot_bf(h, wide[...], NN)
            value = limit(both[:, :q] + (both[:, q:] + dot_bf(l, wide[:, :q], NN)))
            o[now, :] = value.astype(BF)
            gap = limit(y[now, :] - value)
            acc[...] += jnp.sum((gap * gap).reshape(tile // 8, 8, q), axis=0)

        @pl.when(left >= tile)
        def _():
            predict(lambda v: v)

        @pl.when((left > 0) & (left < tile))
        def _():
            keep = lax.broadcasted_iota(jnp.int32, (tile, q), 0) < left
            predict(lambda v: jnp.where(keep, v, 0.0))

        @pl.when(left <= 0)
        def _():
            o[now, :] = jnp.zeros((tile, q), BF)

        out.start()

    share = counts[lax.axis_index("tm")].astype(F32) * q
    e_ref[...] = jnp.broadcast_to(jnp.sum(acc[...]) / share, (1, q))

    @pl.loop(0, tiles)
    def _(k):
        moves(k)[2].wait()


def fit(counts, codes, x, y, given):
    m, f = x.shape
    q = y.shape[1]
    blocks, parts, tile = f // q, len(given), math.gcd(m, 2048)
    smem, vmem, hbm = (pl.BlockSpec(memory_space=s) for s in (pltpu.SMEM, pltpu.VMEM, pl.ANY))
    return pl.pallas_call(
        functools.partial(fit_kernel, blocks=blocks, parts=parts, tile=tile),
        out_shape=(pltpu.HBM((m, q), BF), jax.ShapeDtypeStruct((1, q), F32)),
        in_specs=[smem, smem, hbm, hbm] + [vmem] * parts,
        out_specs=(hbm, vmem),
        scratch_shapes=[
            pltpu.VMEM((m, f), F32),
            pltpu.VMEM((m, q), F32),
            pltpu.VMEM((m, q), BF),
            pltpu.VMEM((f, 2 * q), BF),
            pltpu.VMEM((8, q), F32),
            pltpu.VMEM((parts * given[0].shape[0], q), F32),
            pltpu.VMEM((q, q), F32),
            pltpu.VMEM((32, 32, q), F32),
            pltpu.SemaphoreType.DMA((3, m // tile)),
        ]
        + [pltpu.VMEM((q, q), F32)] * (blocks * (blocks + 1) // 2 + blocks),
        compiler_params=pltpu.CompilerParams(vmem_limit_bytes=FIT_VMEM),
        name="fit",
    )(counts, codes, in_hbm(x), in_hbm(y), *given)


def swap(value, axes, size, j):
    return lax.ppermute(value, axes, [(i, i ^ j) for i in range(size)])


def total(values):
    return functools.reduce(jnp.add, values)


def earlier_sums(mine, sent, n_time, n_rows):
    sub_parts = n_rows
    part_rows = mine.shape[0] // sub_parts
    core_swap = lambda v: swap(v, "rows", n_rows, 1)
    n_seats = n_rows // 2
    time_index = lax.axis_index("tm")
    odd = time_index % 2

    def seat_swap(value, j):
        late, seat = divmod(j, n_seats)
        pairs = [
            (t * n_rows + r, (t ^ late) * n_rows + (r ^ (2 * seat))) for t in range(n_time) for r in range(n_rows)
        ]
        return lax.ppermute(value, ("tm", "rows"), pairs)

    mine = mine + core_swap(sent)
    slots = [mine[j * part_rows : (j + 1) * part_rows] for j in range(sub_parts)]
    slots = [slots[0]] + [seat_swap(slots[j], j) for j in range(1, sub_parts)]
    same, other = total(slots[:n_seats]), total(slots[n_seats:])
    both = same + other
    even_part = jnp.where(odd == 1, other, same)
    group = time_index // 2
    before = jnp.zeros_like(both)
    for j in range(1, n_time // 2):
        came = swap(both, "tm", n_time, 2 * j)
        before = before + jnp.where((group ^ j) < group, came, 0.0)
    with_even = before + even_part
    for_same = jnp.where(odd == 1, with_even, before)
    for_other = jnp.where(odd == 1, before, with_even)
    out = [for_same] + [seat_swap(for_same if j < n_seats else for_other, j) for j in range(1, sub_parts)]
    return out + [core_swap(v) for v in out]


def body(features, response_lines, row_counts, ridge_codes, n_time, n_rows):
    mine, sent = gram(row_counts, features, response_lines, n_rows)
    given = earlier_sums(mine, sent, n_time, n_rows)
    forecast, error = fit(row_counts, ridge_codes, features, response_lines, given)
    partition_mse = total([error] + [swap(error, "rows", n_rows, j) for j in range(1, n_rows)])
    return forecast, partition_mse[0, :1]


def solution(mesh):
    return jax.shard_map(
        functools.partial(body, n_time=mesh.shape["tm"], n_rows=mesh.shape["rows"]),
        mesh=mesh,
        in_specs=(P(("tm", "rows"), None), P(("tm", "rows"), None), P(), P()),
        out_specs=(P(("tm", "rows"), None), P("tm")),
        check_vma=False,
    )
```

```python
import functools
import math

import jax
import jax.numpy as jnp
from jax import lax
from jax.experimental import pallas as pl
from jax.experimental.pallas import tpu as pltpu
from jax.sharding import PartitionSpec as P

GRAM_VMEM, FIT_VMEM = 48 << 20, 48 << 20
BF = jnp.bfloat16
F32 = jnp.float32
NN = (((1,), (0,)), ((), ()))
TN = (((0,), (0,)), ((), ()))


def in_hbm(value):
    return pltpu.with_memory_space_constraint(value, pltpu.HBM)


def split(value):
    high = value.astype(BF)
    return high, (value - high.astype(F32)).astype(BF)


def dot_bf(a, b, dims):
    return lax.dot_general(a, b, dims, preferred_element_type=F32)


def layout(blocks):
    pairs = [("pair", d, d + 1) for d in range(0, blocks - 1, 2)]
    single = [("block", d, d) for d in range(2 * len(pairs), blocks)]
    upper = [("block", i, j) for i in range(blocks) for j in range(i + 1, blocks)]
    return pairs + single + upper + [("block", i, blocks) for i in range(blocks)]


def packed_rows(blocks, q, parts):
    rows = len(layout(blocks)) * q + 8
    return -(-rows // (8 * parts)) * 8 * parts


def seat(n_rows):
    time_index, row_index = lax.axis_index("tm"), lax.axis_index("rows")
    return row_index % 2, (time_index % 2) * (n_rows // 2) + row_index // 2


def valid_rows(counts, m):
    left = counts[lax.axis_index("tm")] - lax.axis_index("rows") * m
    return jnp.minimum(jnp.maximum(left, 0), m)


def gram_kernel(counts, x_hbm, y_hbm, mine_ref, send_ref, x, y, wide, left, cross, sems, *, sub_parts):
    (m, f), q = x.shape, y.shape[1]
    half, blocks = f // 2, f // q
    chunks = sems.shape[1]
    chunk = m // chunks
    part_rows = mine_ref.shape[0] // sub_parts

    def moves(k):
        now = pl.ds(pl.multiple_of(k * chunk, chunk), chunk)
        return (
            pltpu.make_async_copy(x_hbm.at[now, :], x.at[now, :], sems.at[0, k]),
            pltpu.make_async_copy(y_hbm.at[now, :], y.at[now, :], sems.at[1, k]),
        )

    for k in range(chunks):
        for copy in moves(k):
            copy.start()
    for ref in (wide, left, cross):
        ref[...] = jnp.zeros_like(ref)
    valid = valid_rows(counts, m)

    def add(first, count):
        rows = count * chunk
        for k in range(count):
            for copy in moves(first + k):
                copy.wait()
        now = pl.ds(pl.multiple_of(first * chunk, chunk), rows)
        keep = lax.broadcasted_iota(jnp.int32, (rows, 1), 0) < valid - first * chunk
        h, l = split(jnp.where(keep, x[now, :], 0.0))
        yh, yl = split(jnp.where(keep, y[now, :], 0.0))
        wide[...] += dot_bf(h, jnp.concatenate([h[:, half:], l, yh, yl], 1), TN)
        left[...] += dot_bf(h[:, :half], h[:, :half], TN)
        cross[...] += dot_bf(yh, l, TN)

    count = math.gcd(chunks, 4)
    if count == 4:
        add(0, 1)
        add(1, 3)
    else:
        add(0, count)

    @pl.loop(1, chunks // count)
    def _(k):
        add(k * count, count)

    core, place = seat(sub_parts)
    starts = [(sub ^ place) * part_rows for sub in range(sub_parts)]
    row_of = lax.broadcasted_iota(jnp.int32, (q, q), 0)
    col_of = lax.broadcasted_iota(jnp.int32, (q, q), 1)

    def product(i, j):
        si = slice(i * q, (i + 1) * q)
        if j == blocks:
            return wide[si, half + f : half + f + q] + (wide[si, half + f + q :] + cross[:, si].T)
        sj = slice(j * q, (j + 1) * q)
        high = left[si, sj] if (j + 1) * q <= half else wide[si, j * q - half : (j + 1) * q - half]
        return high + (wide[si, half + j * q : half + (j + 1) * q] + wide[sj, half + i * q : half + (i + 1) * q].T)

    def pack(kept_half):
        def put(at, block):
            first, end = at, at + block.shape[0]
            while first < end:
                part, offset = divmod(first, part_rows)
                last = min(end, (part + 1) * part_rows)
                owner, sub = divmod(part, sub_parts)
                target = mine_ref if owner == kept_half else send_ref
                target[pl.ds(pl.multiple_of(starts[sub] + offset, 8), last - first), :] = block[first - at : last - at]
                first = last

        diagonals = []
        for n, (kind, i, j) in enumerate(layout(blocks)):
            if kind == "pair":
                second = product(j, j)
                put(n * q, jnp.where(row_of <= col_of, product(i, i), second))
                diagonals.append(jnp.sum(jnp.where(row_of == col_of, second, 0.0), axis=0, keepdims=True))
            else:
                put(n * q, product(i, j))
        used = len(layout(blocks)) * q
        total_rows = 2 * sub_parts * part_rows
        rest = [jnp.zeros((total_rows - used - len(diagonals), q), F32)]
        put(used, jnp.concatenate(diagonals + rest, 0))

    for c in range(2):
        pl.when(core == c)(functools.partial(pack, c))


def gram(counts, x, y, sub_parts):
    m, f = x.shape
    q = y.shape[1]
    blocks = f // q
    rows = packed_rows(blocks, q, 2 * sub_parts)
    smem, vmem, hbm = (pl.BlockSpec(memory_space=s) for s in (pltpu.SMEM, pltpu.VMEM, pl.ANY))
    return pl.pallas_call(
        functools.partial(gram_kernel, sub_parts=sub_parts),
        out_shape=[jax.ShapeDtypeStruct((rows // 2, q), F32)] * 2,
        in_specs=[smem, hbm, hbm],
        out_specs=[vmem, vmem],
        scratch_shapes=[
            pltpu.VMEM((m, f), F32),
            pltpu.VMEM((m, q), F32),
            pltpu.VMEM((f, f // 2 + f + 2 * q), F32),
            pltpu.VMEM((f // 2, f // 2), F32),
            pltpu.VMEM((q, f), F32),
            pltpu.SemaphoreType.DMA((2, m // math.gcd(m, 512))),
        ],
        compiler_params=pltpu.CompilerParams(vmem_limit_bytes=GRAM_VMEM),
        name="gram",
    )(in_hbm(counts), in_hbm(x), in_hbm(y))


def inverse_factor(groups, kept, span=4):
    count, shape = len(groups), groups[0].shape
    lane = lax.broadcasted_iota(jnp.int32, shape, 1)
    sub = lax.broadcasted_iota(jnp.int32, shape, 0)
    spread = lambda v: jnp.broadcast_to(v, shape)
    out = []
    for k in range(0, count, span):
        c0, width = 8 * k, 8 * span
        inside = (lane >= c0) & (lane < c0 + width)
        col = [[spread(groups[k + g][:, c0 + c : c0 + c + 1]) for c in range(8 * g + 8)] for g in range(span)]
        col[0][0] = col[0][0] + 0.0
        entry = lambda a, b: spread(col[a // 8][b][a % 8 : a % 8 + 1, :])
        pivot = entry(0, 0)
        rows = [
            jnp.where(inside, jnp.where(lane - c0 - 8 * g == sub, 1.0, 0.0), groups[k + g]) for g in range(span)
        ]
        for b in range(width):
            g0, r = divmod(b, 8)
            scale = lax.rsqrt(pivot)
            factor = {g: col[g][b] * scale for g in range(g0, span)}
            for g in range(g0, span):
                kept[b, 8 * g : 8 * g + 8, :] = factor[g]
            if b + 1 < width:
                first = entry(b + 1, b) * scale
                pivot = entry(b + 1, b + 1) - first * first
            for c in range(b + 1, width):
                other = first if c == b + 1 else kept[b, pl.ds(c, 8, stride=0), :]
                for g in range(c // 8, span):
                    col[g][c] = col[g][c] - factor[g] * other
            u = spread(rows[g0][r : r + 1, :]) * scale
            rows[g0] = jnp.where(sub == r, u, rows[g0] - jnp.where(sub > r, factor[g0], 0.0) * u)
            for g in range(g0 + 1, span):
                rows[g] = rows[g] - factor[g] * u
        out += [jnp.where(lane < c0 + width, v, 0.0) for v in rows]
        if k + span < count:
            h, l = split(jnp.concatenate(rows, 0))
            change = dot_bf(jnp.concatenate([h, h, l], 0), jnp.concatenate([h, l, h], 0), TN)
            for g in range(k + span, count):
                groups[g] = jnp.where(inside, 0.0, groups[g]) - change[8 * g : 8 * g + 8]
    return out


def split3(value):
    high = value.astype(BF)
    rest = value - high.astype(F32)
    return (high,) + split(rest)


def dot_six(a, b, dims):
    left = jnp.concatenate([a[i] for i in (0, 0, 1, 0, 2, 1)], dims[0][0][0])
    right = jnp.concatenate([b[i] for i in (0, 1, 0, 2, 0, 1)], dims[0][1][0])
    return dot_bf(left, right, dims)


def solve_into(z, counts, codes, given, packed, linv, kept, tiles):
    parts = len(given)
    sub_parts = parts // 2
    part_rows, q = given[0].shape
    blocks = next(n for n in range(1, len(tiles) + 1) if n * (n + 1) // 2 + n == len(tiles))
    previous = jnp.maximum(lax.axis_index("tm") - 1, 0)
    seen = lax.fori_loop(0, previous + 1, lambda k, t: t + counts[k], jnp.int32(0))
    ridge = codes[previous].astype(F32) * seen.astype(F32) / 16.0
    core, place = seat(sub_parts)
    for slot in range(parts):
        half, sub = divmod(slot, sub_parts)
        part = (half ^ core) * sub_parts + (sub ^ place)
        packed[pl.ds(pl.multiple_of(part * part_rows, 8), part_rows), :] = given[slot][...]
    row_of = lax.broadcasted_iota(jnp.int32, (q, q), 0)
    col_of = lax.broadcasted_iota(jnp.int32, (q, q), 1)
    more = jnp.where(row_of == col_of, ridge, 0.0)
    order = layout(blocks)
    a, pairs = {}, 0
    for n, (kind, i, j) in enumerate(order):
        block = packed[n * q : (n + 1) * q, :]
        if kind == "pair":
            turned = block.T
            at = len(order) * q + pairs
            diagonal = jnp.broadcast_to(packed[at : at + 1, :], (q, q))
            a[i, i], a[j, j] = tiles[2 * pairs], tiles[2 * pairs + 1]
            a[i, i][...] = jnp.where(row_of <= col_of, block, turned) + more
            a[j, j][...] = jnp.where(row_of == col_of, diagonal, jnp.where(row_of > col_of, block, turned)) + more
            pairs += 1
        else:
            a[i, j] = tiles[n + pairs]
            a[i, j][...] = block + more if i == j else block
    for i in range(blocks):
        inverse = inverse_factor([a[i, i][8 * t : 8 * t + 8, :] for t in range(q // 8)], kept)
        for t in range(q // 8):
            linv[8 * t : 8 * t + 8, :] = inverse[t]
        li = split3(linv[...])

        def panel(first, last):
            block = jnp.concatenate([a[i, j][...] for j in range(first, last)], 1)
            return dot_six(li, split3(block), NN)

        pieces = []
        if i + 1 < blocks:
            pieces.append(panel(i + 1, i + 2))
            next_parts = split3(pieces[0])
            a[i + 1, i + 1][...] -= dot_six(next_parts, next_parts, TN)
        pieces.append(panel(i + len(pieces) + 1, blocks + 1))
        row = split3(jnp.concatenate(pieces, 1))
        cut = lambda first, last: [v[:, (first - i - 1) * q : (last - i - 1) * q] for v in row]
        for j in range(i + 1, blocks):
            first = j + 1 if j == i + 1 else j
            change = dot_six(cut(j, j + 1), cut(first, blocks + 1), TN)
            for c in range(first, blocks + 1):
                a[j, c][...] -= change[:, (c - first) * q : (c - first + 1) * q]
        z.append(dot_six(li, row, TN))
        z_parts = split3(z[i])
        for j in range(i):
            z[j] = z[j][:, q:] - dot_six(split3(z[j][:, :q]), z_parts, NN)


def fit_kernel(counts, codes, x_hbm, y_hbm, *refs, parts, blocks, tile):
    given, o_hbm, e_ref = refs[:parts], refs[parts], refs[parts + 1]
    x, y, o, wide, acc, packed, linv, kept, sems = refs[parts + 2 : parts + 11]
    tiles_of_a = refs[parts + 11 :]
    m, q = y.shape
    tiles = m // tile

    def moves(k):
        now = pl.ds(pl.multiple_of(k * tile, tile), tile)
        return (
            pltpu.make_async_copy(x_hbm.at[now, :], x.at[now, :], sems.at[0, k]),
            pltpu.make_async_copy(y_hbm.at[now, :], y.at[now, :], sems.at[1, k]),
            pltpu.make_async_copy(o.at[now, :], o_hbm.at[now, :], sems.at[2, k]),
        )

    for k in range(tiles):
        for copy in moves(k)[:2]:
            copy.start()
    z = []
    solve_into(z, counts, codes, given, packed, linv, kept, tiles_of_a)
    for i in range(blocks):
        here = slice(i * q, (i + 1) * q)
        wide[here, :q], wide[here, q:] = split(z[i])
    acc[...] = jnp.zeros_like(acc)
    valid = valid_rows(counts, m)

    @pl.loop(0, tiles)
    def _(k):
        x_in, y_in, out = moves(k)
        x_in.wait()
        y_in.wait()
        now = pl.ds(pl.multiple_of(k * tile, tile), tile)
        left = valid - k * tile

        def predict(limit):
            h, l = split(x[now, :])
            both = dot_bf(h, wide[...], NN)
            value = limit(both[:, :q] + (both[:, q:] + dot_bf(l, wide[:, :q], NN)))
            o[now, :] = value.astype(BF)
            gap = limit(y[now, :] - value)
            acc[...] += jnp.sum((gap * gap).reshape(tile // 8, 8, q), axis=0)

        @pl.when(left >= tile)
        def _():
            predict(lambda v: v)

        @pl.when((left > 0) & (left < tile))
        def _():
            keep = lax.broadcasted_iota(jnp.int32, (tile, q), 0) < left
            predict(lambda v: jnp.where(keep, v, 0.0))

        @pl.when(left <= 0)
        def _():
            o[now, :] = jnp.zeros((tile, q), BF)

        out.start()

    share = counts[lax.axis_index("tm")].astype(F32) * q
    e_ref[...] = jnp.broadcast_to(jnp.sum(acc[...]) / share, (1, q))

    @pl.loop(0, tiles)
    def _(k):
        moves(k)[2].wait()


def fit(counts, codes, x, y, given):
    m, f = x.shape
    q = y.shape[1]
    blocks, parts, tile = f // q, len(given), math.gcd(m, 2048)
    smem, vmem, hbm = (pl.BlockSpec(memory_space=s) for s in (pltpu.SMEM, pltpu.VMEM, pl.ANY))
    return pl.pallas_call(
        functools.partial(fit_kernel, blocks=blocks, parts=parts, tile=tile),
        out_shape=(pltpu.HBM((m, q), BF), jax.ShapeDtypeStruct((1, q), F32)),
        in_specs=[smem, smem, hbm, hbm] + [vmem] * parts,
        out_specs=(hbm, vmem),
        scratch_shapes=[
            pltpu.VMEM((m, f), F32),
            pltpu.VMEM((m, q), F32),
            pltpu.VMEM((m, q), BF),
            pltpu.VMEM((f, 2 * q), BF),
            pltpu.VMEM((8, q), F32),
            pltpu.VMEM((parts * given[0].shape[0], q), F32),
            pltpu.VMEM((q, q), F32),
            pltpu.VMEM((32, 32, q), F32),
            pltpu.SemaphoreType.DMA((3, m // tile)),
        ]
        + [pltpu.VMEM((q, q), F32)] * (blocks * (blocks + 1) // 2 + blocks),
        compiler_params=pltpu.CompilerParams(vmem_limit_bytes=FIT_VMEM),
        name="fit",
    )(counts, codes, in_hbm(x), in_hbm(y), *given)


def swap(value, axes, size, j):
    return lax.ppermute(value, axes, [(i, i ^ j) for i in range(size)])


def total(values):
    return functools.reduce(jnp.add, values)


def earlier_sums(mine, sent, n_time, n_rows):
    sub_parts = n_rows
    part_rows = mine.shape[0] // sub_parts
    core_swap = lambda v: swap(v, "rows", n_rows, 1)
    n_seats = n_rows // 2
    time_index = lax.axis_index("tm")
    odd = time_index % 2

    def seat_swap(value, j):
        late, seat = divmod(j, n_seats)
        pairs = [
            (t * n_rows + r, (t ^ late) * n_rows + (r ^ (2 * seat))) for t in range(n_time) for r in range(n_rows)
        ]
        return lax.ppermute(value, ("tm", "rows"), pairs)

    mine = mine + core_swap(sent)
    slots = [mine[j * part_rows : (j + 1) * part_rows] for j in range(sub_parts)]
    slots = [slots[0]] + [seat_swap(slots[j], j) for j in range(1, sub_parts)]
    same, other = total(slots[:n_seats]), total(slots[n_seats:])
    both = same + other
    even_part = jnp.where(odd == 1, other, same)
    group = time_index // 2
    before = jnp.zeros_like(both)
    for j in range(1, n_time // 2):
        came = swap(both, "tm", n_time, 2 * j)
        before = before + jnp.where((group ^ j) < group, came, 0.0)
    with_even = before + even_part
    for_same = jnp.where(odd == 1, with_even, before)
    for_other = jnp.where(odd == 1, before, with_even)
    out = [for_same] + [seat_swap(for_same if j < n_seats else for_other, j) for j in range(1, sub_parts)]
    return out + [core_swap(v) for v in out]


def body(features, response_lines, row_counts, ridge_codes, n_time, n_rows):
    mine, sent = gram(row_counts, features, response_lines, n_rows)
    given = earlier_sums(mine, sent, n_time, n_rows)
    forecast, error = fit(row_counts, ridge_codes, features, response_lines, given)
    partition_mse = total([error] + [swap(error, "rows", n_rows, j) for j in range(1, n_rows)])
    return forecast, partition_mse[0, :1]


def solution(mesh):
    return jax.shard_map(
        functools.partial(body, n_time=mesh.shape["tm"], n_rows=mesh.shape["rows"]),
        mesh=mesh,
        in_specs=(P(("tm", "rows"), None), P(("tm", "rows"), None), P(), P()),
        out_specs=(P(("tm", "rows"), None), P("tm")),
        check_vma=False,
    )
```
